256 devices in a mesh: dp: 8 (over y, core), tensor: 32 (over x, z).
Axes of the slice: x: 4, y: 4, z: 8, core: 2. Of those that a mesh axis runs over, the one named last changes fastest.
Arguments:
- tokens: bfloat16 [2048, 8192], P('dp', 'tensor'), may hold values from -6 to 6
- pattern: int32 [256, 8], P('tensor'), may hold values from 0 to 63, as said below
- first_blocks: bfloat16 [256, 8, 128, 128], P('tensor'), may hold values from -0.1875 to 0.1875
- second_blocks: bfloat16 [256, 8, 128, 128], P('tensor'), may hold values from -0.1875 to 0.1875
- out_grad: bfloat16 [2048, 8192], P('dp', 'tensor'), may hold values from -0.75 to 0.75
Outputs:
- layer_out: bfloat16 [2048, 8192], P('dp', 'tensor')
- input_grad: bfloat16 [2048, 8192], P('dp', 'tensor')
- first_grad: bfloat16 [256, 8, 128, 128], P('tensor')
- second_grad: bfloat16 [256, 8, 128, 128], P('tensor')
The draws below stay inside these ranges and needn't reach their ends.
Inputs may be any that keep to these rules, and one draw needn't show every extreme that they name: `pattern`: each hidden block row r lists 8 distinct feature blocks: r mod 64, the blocks that differ from it in bit 0, in bit 3 and in the highest bit, and 4 further ones drawn at random. Every feature block is listed by some row.
All inputs are finite; a program needn't handle non-finite values.
Results may differ from the reference program's by a relative error of at most 0.015.
Values may be sent and summed in bfloat16 or wider, within the bound.
A program may use at most 128 MiB of HBM per device.

```python
import jax
import jax.numpy as jnp
from jax import lax

D = 8192
BLK = 128
K = 8
TOK_DEV = 256
FB = 64
HB = 256
TOKENS = 2048
N_DP = 8
N_TENSOR = 32


def draw_pattern(key, part):
    row_ids = jnp.arange(HB, dtype=jnp.int32)
    base = row_ids % FB
    fixed_cols = jnp.stack([base, base ^ 1, base ^ 8, base ^ FB // 2], axis=1)
    columns = jnp.arange(FB, dtype=jnp.int32)
    scores = jax.random.randint(key, (HB, FB), 0, 1 << 20, dtype=jnp.int32) * FB + columns[None, :]
    taken = jnp.any(fixed_cols[:, :, None] == columns[None, None, :], axis=1)
    scores = jnp.where(taken, -1, scores)
    _, extra = lax.top_k(scores, K - 4)
    return jnp.concatenate([fixed_cols, extra.astype(jnp.int32)], axis=1).astype(jnp.int32)


def steps_of(key, extent, split, smallest, largest):
    def one(position, shards_of):
        heights = jax.random.uniform(jax.random.fold_in(jax.random.fold_in(key, 6), position), (shards_of,), jnp.float32, smallest / len(split), largest / len(split))
        return jnp.repeat(jnp.exp(heights), extent[position] // shards_of).reshape((-1,) + (1,) * (len(extent) - position - 1))

    level = one(*split[0])
    for cut in split[1:]:
        level = level * one(*cut)
    return level


def scatter_about(stream_key, dims, width, most, pieces=(), kind=jnp.bfloat16):
    gain = steps_of(stream_key, dims, pieces, -0.22, 0.18) if pieces else 1.0
    array = jax.random.normal(stream_key, dims, jnp.float32) * width * gain
    return jnp.minimum(jnp.maximum(array, -most), most).astype(kind)


def setup_inputs(seed: int = 0) -> dict:
    arg_keys = jax.random.split(jax.random.key(seed), 6)
    return {
        "tokens": scatter_about(arg_keys[0], (TOKENS, D), 1.0, 6.0, ((0, 8), (1, 32))),
        "pattern": draw_pattern(jax.random.fold_in(arg_keys[5], 71), 0),
        "first_blocks": scatter_about(arg_keys[2], (HB, K, BLK, BLK), (K * BLK) ** -0.5, 0.1875, ((0, 32),)),
        "second_blocks": scatter_about(arg_keys[3], (HB, K, BLK, BLK), (K * BLK) ** -0.5, 0.1875, ((0, 32),)),
        "out_grad": scatter_about(arg_keys[4], (TOKENS, D), 0.125, 0.75, ((0, 8), (1, 32))),
    }


gelu_scale = 0.7978845608028654
gelu_cube = 0.044715


def gelu_pair(value):
    inner = gelu_scale * (value + gelu_cube * value * value * value)
    tangent = jnp.tanh(inner)
    result = 0.5 * value * (1.0 + tangent)
    slope = 0.5 * (1.0 + tangent) + 0.5 * value * (1.0 - tangent * tangent) * gelu_scale * (1.0 + 3.0 * gelu_cube * value * value)
    return result, slope


def rounded(value):
    return lax.optimization_barrier(value.astype(jnp.bfloat16)).astype(jnp.float32)


def reference(tokens, pattern, first_blocks, second_blocks, out_grad):
    highest = lax.Precision.HIGHEST
    features = tokens.reshape(N_DP, TOK_DEV, FB, BLK)
    grads = out_grad.reshape(N_DP, TOK_DEV, FB, BLK)
    group_rows = HB // N_TENSOR
    pattern_groups = pattern.reshape(N_TENSOR, group_rows, K)
    first_groups = first_blocks.reshape(N_TENSOR, group_rows, K, BLK, BLK)
    second_groups = second_blocks.reshape(N_TENSOR, group_rows, K, BLK, BLK)
    columns = jnp.arange(FB, dtype=jnp.int32)

    def step(carry, item):
        out_total, back_total = carry
        rows_pattern, first_part, second_part = item
        first_wide = first_part.astype(jnp.float32)
        second_wide = second_part.astype(jnp.float32)
        select = (rows_pattern[:, :, None] == columns).astype(jnp.float32)
        picked = features[:, :, rows_pattern, :].astype(jnp.float32)
        pre = jnp.einsum('gtrki,rkio->gtro', picked, first_wide)
        value, slope = gelu_pair(pre)
        active = rounded(value)
        contrib = jnp.einsum('gtro,rkoc->gtrkc', active, second_wide)
        out_part = jnp.einsum('gtrkc,rkf->gtfc', contrib, select, precision=highest)
        out_total = out_total + rounded(out_part)
        grad_picked = grads[:, :, rows_pattern, :].astype(jnp.float32)
        act_grad = jnp.einsum('gtrkc,rkoc->gtro', grad_picked, second_wide)
        pre_grad = rounded(act_grad * slope)
        second_term = jnp.sum(rounded(jnp.einsum('gtro,gtrkc->grkoc', active, grad_picked)), axis=0).astype(jnp.bfloat16)
        first_term = jnp.sum(rounded(jnp.einsum('gtrki,gtro->grkio', picked, pre_grad)), axis=0).astype(jnp.bfloat16)
        back_term = jnp.einsum('gtro,rkio->gtrki', pre_grad, first_wide)
        back_part = jnp.einsum('gtrki,rkf->gtfi', back_term, select, precision=highest)
        back_total = back_total + rounded(back_part)
        return (out_total, back_total), (first_term, second_term)

    start = jnp.zeros((N_DP, TOK_DEV, FB, BLK), jnp.float32)
    (out_total, back_total), (first_all, second_all) = lax.scan(step, (start, start), (pattern_groups, first_groups, second_groups))
    layer_out = out_total.reshape(N_DP * TOK_DEV, FB * BLK).astype(jnp.bfloat16)
    input_grad = back_total.reshape(N_DP * TOK_DEV, FB * BLK).astype(jnp.bfloat16)
    first_grad = first_all.reshape(HB, K, BLK, BLK)
    second_grad = second_all.reshape(HB, K, BLK, BLK)
    return (layer_out, input_grad, first_grad, second_grad)
```

```python
import heapq

import jax
import jax.numpy as jnp
from jax import lax
from jax.experimental import pallas as pl
from jax.experimental.pallas import tpu as pltpu
from jax.sharding import PartitionSpec as P

MESH = pl.DeviceIdType.MESH
BF = jnp.bfloat16
F32 = jnp.float32

gelu_scale = 0.7978845608028654
gelu_cube = 0.044715

NX, NZ, NY = 4, 8, 4
ROWS, BLK, HR, K = 256, 128, 8, 8
RA = 96
RB = ROWS - RA
SIGNS = (1, -1)


UNIT = 2.8
LAT = 1.6
GB2 = UNIT


def build_items():
    items = {}

    def add(key, link, size, deps):
        items[key] = (link, size, tuple(deps))

    fa, fb = RA / ROWS, RB / ROWS

    def name(axis, s):
        return axis + ("+" if s > 0 else "-")

    for p in (0, 1):
        gate = [("gate", "ag", p)]
        for s in SIGNS:
            add(("bz", p, s, 1), name("z", s), fb, gate)
            add(("ax", p, s, 1), name("x", s), fa, gate)
        for s in SIGNS:
            add(("az", p, 0, s, 1), name("z", s), fa, gate)
            add(("bx", p, 0, s, 1), name("x", s), fb, gate)
        for s in SIGNS:
            add(("ax", p, s, 2), name("x", s), fa / 2, [("ax", p, s, 1)])
            for k in (2, 3, 4):
                add(("bz", p, s, k), name("z", s), fb if k < 4 else fb / 2, [("bz", p, s, k - 1)])
        for dx, ready in (
            (0, gate),
            (-1, [("ax", p, 1, 1)]),
            (1, [("ax", p, -1, 1)]),
            (2, [("ax", p, 1, 2), ("ax", p, -1, 2)]),
        ):
            for s in SIGNS:
                for k in (1, 2, 3, 4):
                    add(
                        ("az", p, dx, s, k),
                        name("z", s),
                        fa if k < 4 else fa / 2,
                        ready if k == 1 else [("az", p, dx, s, k - 1)],
                    )
        for dz in (0, -1, 1, -2, 2, -3, 3, 4):
            if dz == 0:
                ready = gate
            elif dz == 4:
                ready = [("bz", p, 1, 4), ("bz", p, -1, 4)]
            else:
                ready = [("bz", p, 1 if dz < 0 else -1, abs(dz))]
            for s in SIGNS:
                add(("bx", p, dz, s, 1), name("x", s), fb, ready)
                add(("bx", p, dz, s, 2), name("x", s), fb / 2, [("bx", p, dz, s, 1)])
    for q in (0, 1):
        gate = [("gate", "rs", q)]

        def done_a(dx):
            return [("rz", q, dx, s, 1) for s in SIGNS]

        def done_b(dz):
            return [("sx", q, dz, s, 1) for s in SIGNS]

        for dx in (2, 1, -1, 0):
            for s in SIGNS:
                for k in (4, 3, 2, 1):
                    add(
                        ("rz", q, dx, s, k),
                        name("z", s),
                        fa if k < 4 else fa / 2,
                        gate if k == 4 else [("rz", q, dx, s, k + 1)],
                    )
        for dz in (4, 3, -3, 2, -2, 1, -1, 0):
            for s in SIGNS:
                add(("sx", q, dz, s, 2), name("x", s), fb / 2, gate)
                add(("sx", q, dz, s, 1), name("x", s), fb, [("sx", q, dz, s, 2)])
        for s in SIGNS:
            add(("rx", q, s, 2), name("x", s), fa / 2, done_a(2))
            add(("rx", q, s, 1), name("x", s), fa, [("rx", q, s, 2)] + done_a(s))
            add(("sz", q, s, 4), name("z", s), fb / 2, done_b(4))
            for k in (3, 2, 1):
                add(("sz", q, s, k), name("z", s), fb, [("sz", q, s, k + 1)] + done_b(s * k))
    for m in (0, 1):
        add(("pc", m), "c", 1.6, [("grad", m)])
        for s in SIGNS:
            add(("yr", m, s, 2), name("y", s), 1.0, [("pc", m)])
            add(("yr", m, s, 1), name("y", s), 2.0, [("yr", m, s, 2)])
        fin = [("yr", m, s, 1) for s in SIGNS]
        for s in SIGNS:
            add(("yg", m, s, 1), name("y", s), 2.0, fin)
            add(("yg", m, s, 2), name("y", s), 1.0, [("yg", m, s, 1)])
        add(("cg", m, 0), "c", 0.4, fin)
        add(("cg", m, -1), "c", 0.4, [("yg", m, 1, 1)])
        add(("cg", m, 1), "c", 0.4, [("yg", m, -1, 1)])
        add(("cg", m, 2), "c", 0.4, [("yg", m, 1, 2), ("yg", m, -1, 2)])
    return items


def build_chunks(items):
    def all_of(kinds, p):
        return [k for k in items if k[0] in kinds and k[1] == p]

    ag = ("ax", "az", "bz", "bx")
    chunks = [(("load",), 0.5, [("count", "ag", 0, 30)])]
    chunks += [(("pre", i), 1.5, all_of(ag, 0) + [("load",)]) for i in range(4)]
    pre = [("pre", i) for i in range(4)]
    chunks += [(("out", i), 1.0, pre) for i in range(8)]
    chunks += [(("sterm", i), 1.2, all_of(ag, 1) + pre) for i in range(4)]
    chunks += [(("agrad", i), 1.5, all_of(ag, 1) + pre) for i in range(4)]
    agr = [("agrad", i) for i in range(4)]
    chunks += [(("fterm", i), 1.4, agr) for i in range(4)]
    chunks += [(("back", i), 1.0, agr) for i in range(8)]
    return chunks


def build_marks(items):
    final = [
        [("rx", q, s, 1) for s in SIGNS]
        + [("rz", q, 0, s, 1) for s in SIGNS]
        + [("sz", q, s, 1) for s in SIGNS]
        + [("sx", q, 0, s, 1) for s in SIGNS]
        for q in (0, 1)
    ]
    marks = [
        (("gate", "ag", 0), []),
        (("gate", "ag", 1), [("count", "ag", 0, 62)]),
        (("gate", "rs", 0), [("out", i) for i in range(8)] + [("count", "ag", 1, 62)]),
        (("gate", "rs", 1), [("back", i) for i in range(8)] + [("count", "rs", 0, 62)]),
        (("grad", 0), [("sterm", i) for i in range(4)]),
        (("grad", 1), [("fterm", i) for i in range(4)]),
        (("store", 0), final[0]),
        (("store", 1), final[1]),
        (("own", 0), [("yr", 0, s, 1) for s in SIGNS]),
        (("own", 1), [("yr", 1, s, 1) for s in SIGNS]),
    ]
    return marks


GROUP = {k: "ag" for k in ("ax", "az", "bz", "bx")} | {k: "rs" for k in ("rz", "rx", "sx", "sz")}
COST = {"ag": 0.03, "rs": 0.15}


def build_order():
    items = build_items()
    chunks = build_chunks(items)
    marks = build_marks(items)
    got, counts, free = set(), {}, {}
    waiting = list(items)
    heap, order = [], []
    now, seq = 0.0, 0

    def met(need):
        if need[0] == "count":
            return counts.get((need[1], need[2]), 0) >= need[3]
        return need in got

    def settle():
        nonlocal now, seq
        moved = True
        while moved:
            moved = False
            for mark in list(marks):
                if all(met(n) for n in mark[1]):
                    marks.remove(mark)
                    order.append(("mark", mark[0]))
                    got.add(mark[0])
                    moved = True
            for key in list(waiting):
                link, size, deps = items[key]
                if all(d in got for d in deps):
                    waiting.remove(key)
                    order.append(("send", key))
                    now += 0.03
                    start = max(now, free.get(link, 0.0))
                    free[link] = start + size * UNIT
                    seq += 1
                    heapq.heappush(heap, (free[link] + LAT, seq, key))
                    moved = True

    settle()
    while heap or chunks:
        if heap and heap[0][0] <= now:
            key = heapq.heappop(heap)[2]
            order.append(("recv", key))
            got.add(key)
            group = GROUP.get(key[0], "ar")
            counts[(group, key[1])] = counts.get((group, key[1]), 0) + 1
            now += COST.get(group, 0.3)
            settle()
            continue
        if chunks and all(met(n) for n in chunks[0][2]):
            key, time, _ = chunks.pop(0)
            order.append(("comp", key))
            got.add(key)
            now += time
            settle()
            continue
        now = max(now, heap[0][0])
    assert not waiting and not marks
    return list(items), order, now


KEYS, ORDER, SPAN = build_order()
INDEX = {k: i for i, k in enumerate(KEYS)}


def slot_index():
    a, b, y = {}, {}, {}
    for k in KEYS:
        if k[0] in ("rz", "rx") and k[1] == 0:
            a[(k[0],) + k[2:]] = len(a)
        if k[0] in ("sx", "sz") and k[1] == 0:
            b[(k[0],) + k[2:]] = len(b)
        if k[0] == "yr" and k[1] == 0:
            y[k[2:]] = len(y)
    return a, b, y


SLOT_A, SLOT_B, SLOT_Y = slot_index()


def gelu_pair(value):
    inner = gelu_scale * (value + gelu_cube * value * value * value)
    tangent = jnp.tanh(inner)
    result = 0.5 * value * (1.0 + tangent)
    slope = 0.5 * (1.0 + tangent) + 0.5 * value * (1.0 - tangent * tangent) * gelu_scale * (
        1.0 + 3.0 * gelu_cube * value * value
    )
    return result, slope


def kernel(
    tokens, grads, patv, pats, first, second,
    out_ref, back_ref, fgrad_ref, sgrad_ref,
    xb, gb, part0, part1, slot_a, slot_b, w1, w2, act, pgrad, slope_ref,
    sgr, fgr, pair, yslot, invv, invs,
    send_sem, recv_sem, local_sem,
):
    t = lax.axis_index("tensor")
    d = lax.axis_index("dp")
    x, z = lax.div(t, NZ), lax.rem(t, NZ)
    y, core = lax.div(d, 2), lax.rem(d, 2)

    def at(dx, dz):
        return lax.rem(x + (dx + NX), NX) * NZ + lax.rem(z + (dz + NZ), NZ)

    def dev_x(s):
        return {"tensor": at(s, 0)}

    def dev_z(s):
        return {"tensor": at(0, s)}

    def dev_y(s):
        return {"dp": lax.rem(y + (s + NY), NY) * 2 + core}

    partner = {"dp": y * 2 + (1 - core)}
    base = core * 4

    def yrow(dy, b=None):
        return (base if b is None else b) + lax.rem(y + (dy + NY), NY)

    barrier = pltpu.get_barrier_semaphore()
    for dev in (dev_x(1), dev_x(-1), dev_z(1), dev_z(-1), dev_y(1), dev_y(-1), partner):
        pl.semaphore_signal(barrier, inc=1, device_id=dev, device_id_type=MESH)

    local = []
    for n, (src, buf) in enumerate(((tokens, xb), (grads, gb))):
        for h in (0, 1):
            c = pltpu.make_async_copy(
                src.at[:, pl.ds(h * BLK, BLK)], buf.at[t, h], local_sem.at[2 * n + h]
            )
            c.start()
            local.append(c)
    load_w1 = pltpu.make_async_copy(first, w1.at[:, pl.ds(0, K)], local_sem.at[4])
    load_w2 = pltpu.make_async_copy(second, w2.at[:, pl.ds(0, K)], local_sem.at[5])
    load_w1.start()
    load_w2.start()

    cols = lax.broadcasted_iota(jnp.int32, (HR, BLK), 1)
    inv = jnp.full((HR, BLK), K, jnp.int32)
    for j in range(K):
        inv = jnp.where(patv[:, j : j + 1] == cols, j, inv)
    invv[...] = inv
    load_inv = pltpu.make_async_copy(invv, invs, local_sem.at[6])
    load_inv.start()
    for c in local:
        c.wait()

    pl.semaphore_wait(barrier, 7)

    gathered = (xb, gb)
    parts = (part0, part1)
    grad_of = (sgr, fgr)
    grad_out = (sgrad_ref, fgrad_ref)
    rows_a, rows_b = pl.ds(0, RA), pl.ds(RA, RB)

    def half(s):
        return 0 if s > 0 else 1

    def copy_of(key, sent=True):
        kind = key[0]
        i = INDEX[key]
        ss, rs = send_sem.at[i], recv_sem.at[i]

        def remote(src, dst, dev):
            return pltpu.make_async_remote_copy(
                src_ref=src, dst_ref=dst, send_sem=ss, recv_sem=rs, device_id=dev, device_id_type=MESH
            )

        if kind in ("ax", "az", "bz", "bx"):
            buf = gathered[key[1]]
            s, k = key[-2], key[-1]
            rows = rows_a if kind[0] == "a" else rows_b
            if kind == "ax":
                own, got, dev, split = at(-s * (k - 1), 0), at(-s * k, 0), dev_x(s), k == 2
            elif kind == "az":
                dx = key[2]
                own, got, dev, split = at(dx, -s * (k - 1)), at(dx, -s * k), dev_z(s), k == 4
            elif kind == "bz":
                own, got, dev, split = at(0, -s * (k - 1)), at(0, -s * k), dev_z(s), k == 4
            else:
                dz = key[2]
                own, got, dev, split = at(-s * (k - 1), dz), at(-s * k, dz), dev_x(s), k == 2
            hs = pl.ds(half(s), 1) if split else pl.ds(0, 2)

            def view(shard):
                return buf.at[shard, hs, rows, :]

            shard = own if sent else got
            return remote(view(shard), view(shard), dev)
        if kind in ("rz", "rx", "sx", "sz"):
            q, s, k = key[1], key[-2], key[-1]
            buf = parts[q]
            sub = (kind,) + key[2:]
            if kind[0] == "r":
                rows, slot = rows_a, slot_a.at[q, SLOT_A[sub]]
            else:
                rows, slot = rows_b, slot_b.at[q, SLOT_B[sub]]
            if kind == "rz":
                own, dev, split = at(key[2], s * k), dev_z(s), k == 4
            elif kind == "sz":
                own, dev, split = at(0, s * k), dev_z(s), k == 4
            elif kind == "rx":
                own, dev, split = at(s * k, 0), dev_x(s), k == 2
            else:
                own, dev, split = at(s * k, key[2]), dev_x(s), k == 2
            hs = pl.ds(half(s), 1) if split else pl.ds(0, 2)
            return remote(buf.at[own, hs, rows, :], slot.at[hs], dev)
        m = key[1]
        g, out = grad_of[m], grad_out[m]
        if kind == "pc":
            return remote(g.at[pl.ds((1 - core) * 4, 4)], pair.at[m], partner)
        if kind == "yr":
            s, k = key[2], key[3]
            js = pl.ds(half(s) * 4, 4) if k == 2 else pl.ds(0, 8)
            return remote(g.at[yrow(s * k), js], yslot.at[m, SLOT_Y[(s, k)], js], dev_y(s))
        if kind == "yg":
            s, k = key[2], key[3]
            js = pl.ds(half(s) * 4, 4) if k == 2 else pl.ds(0, 8)
            if not sent:
                got = out.at[yrow(-s * k), js]
                return remote(got, got, dev_y(s))
            src = g.at[yrow(0), js] if k == 1 else out.at[yrow(-s), js]
            return remote(src, out.at[yrow(-s * (k - 1)), js], dev_y(s))
        dy = key[2]
        if not sent:
            got = out.at[yrow(dy, (1 - core) * 4)]
            return remote(got, got, partner)
        src = g.at[yrow(0)] if dy == 0 else out.at[yrow(dy)]
        return remote(src, out.at[yrow(dy)], partner)

    def received(key):
        kind = key[0]
        copy_of(key, sent=False).wait_recv()
        if kind in ("rz", "rx", "sx", "sz"):
            q, s, k = key[1], key[-2], key[-1]
            buf = parts[q]
            sub = (kind,) + key[2:]
            if kind[0] == "r":
                rows, slot = rows_a, slot_a.at[q, SLOT_A[sub]]
            else:
                rows, slot = rows_b, slot_b.at[q, SLOT_B[sub]]
            if kind == "rz":
                mine, split = at(key[2], s * (k - 1)), k == 4
            elif kind == "sz":
                mine, split = at(0, s * (k - 1)), k == 4
            elif kind == "rx":
                mine, split = at(s * (k - 1), 0), k == 2
            else:
                mine, split = at(s * (k - 1), key[2]), k == 2
            for h in (half(s),) if split else (0, 1):
                total = buf[mine, h, rows, :].astype(F32) + slot[h].astype(F32)
                buf[mine, h, rows, :] = total.astype(BF)
        elif kind == "pc":
            m = key[1]
            g = grad_of[m]

            @pl.loop(0, 4)
            def _(r):
                @pl.loop(0, K)
                def _(j):
                    total = g[base + r, j].astype(F32) + pair[m, r, j].astype(F32)
                    g[base + r, j] = total.astype(BF)
        elif kind == "yr":
            m, s, k = key[1:]
            g = grad_of[m]
            lo, n = (half(s) * 4, 4) if k == 2 else (0, 8)
            row = yrow(s * (k - 1))

            @pl.loop(lo, lo + n)
            def _(j):
                total = g[row, j].astype(F32) + yslot[m, SLOT_Y[(s, k)], j].astype(F32)
                g[row, j] = total.astype(BF)

    def picked(buf, r):
        return jnp.concatenate([buf[lax.div(pats[r, j], 2), lax.rem(pats[r, j], 2)] for j in range(K)], axis=1)

    def whole(ref):
        return jnp.concatenate([ref[r] for r in range(HR)], axis=1)

    nt = (((1,), (1,)), ((), ()))

    def compute(key):
        kind = key[0]
        if kind == "load":
            load_w1.wait()
            load_w2.wait()
            load_inv.wait()
            for w in (w1, w2):
                for r in range(HR):
                    w[r, K] = jnp.zeros((BLK, BLK), BF)
            return
        i = key[1]
        if kind in ("out", "back"):

            @pl.loop(i * 4, i * 4 + 4)
            def _(dest):
                if kind == "out":
                    rhs = jnp.concatenate(
                        [
                            jnp.concatenate([w2[r, invs[r, 2 * dest + h]] for r in range(HR)], axis=0)
                            for h in (0, 1)
                        ],
                        axis=1,
                    )
                    res = jnp.dot(whole(act), rhs, preferred_element_type=F32)
                else:
                    rhs = jnp.concatenate(
                        [
                            jnp.concatenate([w1[r, invs[r, 2 * dest + h]] for r in range(HR)], axis=1)
                            for h in (0, 1)
                        ],
                        axis=0,
                    )
                    res = lax.dot_general(whole(pgrad), rhs, nt, preferred_element_type=F32)
                buf = part0 if kind == "out" else part1
                for h in (0, 1):
                    buf[dest, h] = res[:, h * BLK : (h + 1) * BLK].astype(BF)

            return

        @pl.loop(i * 2, i * 2 + 2)
        def _(r):
            if kind == "pre":
                weights = jnp.concatenate([w1[r, j] for j in range(K)], axis=0)
                pre = jnp.dot(picked(xb, r), weights, preferred_element_type=F32)
                value, slope = gelu_pair(pre)
                act[r] = value.astype(BF)
                slope_ref[r] = slope
            elif kind == "sterm":
                res = jnp.dot(act[r].T, picked(gb, r), preferred_element_type=F32)
                for j in range(K):
                    sgr[r, j] = res[:, j * BLK : (j + 1) * BLK].astype(BF)
            elif kind == "agrad":
                weights = jnp.concatenate([w2[r, j] for j in range(K)], axis=1)
                res = lax.dot_general(picked(gb, r), weights, nt, preferred_element_type=F32)
                pgrad[r] = (res * slope_ref[r]).astype(BF)
            elif kind == "fterm":
                res = jnp.dot(pgrad[r].T, picked(xb, r), preferred_element_type=F32)
                for j in range(K):
                    fgr[r, j] = res[:, j * BLK : (j + 1) * BLK].astype(BF).T

    stores = []

    def store(src, dst):
        c = pltpu.make_async_copy(src, dst, local_sem.at[8 + len(stores)])
        c.start()
        stores.append(c)

    def marked(key):
        if key[0] == "store":
            q = key[1]
            dst = (out_ref, back_ref)[q]
            for h in (0, 1):
                store(parts[q].at[t, h], dst.at[:, pl.ds(h * BLK, BLK)])
        elif key[0] == "own":
            m = key[1]
            store(grad_of[m].at[yrow(0)], grad_out[m].at[yrow(0)])

    for action, key in ORDER:
        if action == "send":
            copy_of(key).start()
        elif action == "recv":
            received(key)
        elif action == "comp":
            compute(key)
        else:
            marked(key)
    for key in KEYS:
        copy_of(key).wait_send()
    for c in stores:
        c.wait()


def shards(tokens, pattern, first_blocks, second_blocks, out_grad):
    any_space = pl.BlockSpec(memory_space=pl.ANY)
    n = len(KEYS)
    return pl.pallas_call(
        kernel,
        out_shape=(
            jax.ShapeDtypeStruct(tokens.shape, BF),
            jax.ShapeDtypeStruct(tokens.shape, BF),
            jax.ShapeDtypeStruct(first_blocks.shape, BF),
            jax.ShapeDtypeStruct(second_blocks.shape, BF),
        ),
        in_specs=[
            any_space,
            any_space,
            pl.BlockSpec(memory_space=pltpu.VMEM),
            pl.BlockSpec(memory_space=pltpu.SMEM),
            any_space,
            any_space,
        ],
        out_specs=(any_space,) * 4,
        scratch_shapes=[
            pltpu.VMEM((32, 2, ROWS, BLK), BF),
            pltpu.VMEM((32, 2, ROWS, BLK), BF),
            pltpu.VMEM((32, 2, ROWS, BLK), BF),
            pltpu.VMEM((32, 2, ROWS, BLK), BF),
            pltpu.VMEM((2, len(SLOT_A), 2, RA, BLK), BF),
            pltpu.VMEM((2, len(SLOT_B), 2, RB, BLK), BF),
            pltpu.VMEM((HR, K + 1, BLK, BLK), BF),
            pltpu.VMEM((HR, K + 1, BLK, BLK), BF),
            pltpu.VMEM((HR, ROWS, BLK), BF),
            pltpu.VMEM((HR, ROWS, BLK), BF),
            pltpu.VMEM((HR, ROWS, BLK), F32),
            pltpu.VMEM((HR, K, BLK, BLK), BF),
            pltpu.VMEM((HR, K, BLK, BLK), BF),
            pltpu.VMEM((2, 4, K, BLK, BLK), BF),
            pltpu.VMEM((2, 4, K, BLK, BLK), BF),
            pltpu.VMEM((HR, BLK), jnp.int32),
            pltpu.SMEM((HR, BLK), jnp.int32),
            pltpu.SemaphoreType.DMA((n,)),
            pltpu.SemaphoreType.DMA((n,)),
            pltpu.SemaphoreType.DMA((16,)),
        ],
        compiler_params=pltpu.CompilerParams(
            collective_id=0, has_side_effects=True, vmem_limit_bytes=62 * 1024 * 1024
        ),
    )(tokens, out_grad, pattern, pattern, first_blocks, second_blocks)


def solution(mesh):
    placed = (
        P("dp", "tensor"),
        P("tensor", None),
        P("tensor", None, None, None),
        P("tensor", None, None, None),
        P("dp", "tensor"),
    )
    return jax.shard_map(
        shards,
        mesh=mesh,
        in_specs=placed,
        out_specs=(
            P("dp", "tensor"),
            P("dp", "tensor"),
            P("tensor", None, None, None),
            P("tensor", None, None, None),
        ),
        check_vma=False,
    )
```

```python
import heapq

import jax
import jax.numpy as jnp
from jax import lax
from jax.experimental import pallas as pl
from jax.experimental.pallas import tpu as pltpu
from jax.sharding import PartitionSpec as P

MESH = pl.DeviceIdType.MESH
BF = jnp.bfloat16
F32 = jnp.float32

gelu_scale = 0.7978845608028654
gelu_cube = 0.044715

NX, NZ, NY = 4, 8, 4
ROWS, BLK, HR, K = 256, 128, 8, 8
RA = 96
RB = ROWS - RA
SIGNS = (1, -1)


OPT = dict(
    ra=(RA, RA, RA, RA), UNIT=2.7, LAT=1.9, g1=56, g2=66, g3=36, dzs=(4, 3, -3, 2, -2, 1, -1, 0), dxs=(2, 1, -1, 0),
    pf=0, ps=-1, cl=1.6, h=4, late_dz=(), late_dx=(0, 1, -1),
)
GROUP = {k: "ag" for k in ("ax", "az", "bz", "bx")} | {k: "rs" for k in ("rz", "rx", "sx", "sz")}
COST = {"ag": 0.03, "rs": 0.22}


def name(axis, s):
    return axis + ("+" if s > 0 else "-")


DZ=(4,3,-3,2,-2,1,-1,0)
def nz(dz): return 4 if dz==-4 else dz
def pair_of(key):
    if key[0]=="pc": return key
    if key[0]=="cg": return key[:2]
    return key[:-2]+key[-1:]
def recv_need(key):
    kind="out" if key[1]==0 else "back"
    if key[0] in ("rz","sz"): return [(kind, nz(c*(key[-1]-1))) for c in SIGNS]
    if key[0]=="rx": return [(kind,0)]
    if key[0]=="sx": return [(kind,key[2])]
    if key[0]=="pc": return [("grad",key[1],2)]
    return []
def build_items(o):
    items={}
    def add(key, link, size, deps): items[key]=(link,size,tuple(deps))
    for p in (0, 1):
        gate = [("gate", "ag", p)]
        fa = o["ra"][p] / ROWS
        fb = 1 - fa
        for s in SIGNS:
            add(("bz", p, s, 1), name("z", s), fb, gate)
            add(("ax", p, s, 1), name("x", s), fa, gate)
        for s in SIGNS:
            add(("az", p, 0, s, 1), name("z", s), fa, gate)
            add(("bx", p, 0, s, 1), name("x", s), fb, gate)
        for s in SIGNS:
            add(("ax", p, s, 2), name("x", s), fa / 2, [("ax", p, s, 1)])
            for k in (2, 3, 4):
                add(("bz", p, s, k), name("z", s), fb if k < 4 else fb / 2, [("bz", p, s, k - 1)])
        for dx, ready in ((0, gate),(-1, [("ax", p, 1, 1)]),(1, [("ax", p, -1, 1)]),(2, [("ax", p, 1, 2), ("ax", p, -1, 2)])):
            for s in SIGNS:
                for k in (1, 2, 3, 4):
                    add(("az", p, dx, s, k), name("z", s), fa if k < 4 else fa / 2, ready if k == 1 else [("az", p, dx, s, k - 1)])
        for dz in (0, -1, 1, -2, 2, -3, 3, 4):
            if dz == 0: ready = gate
            elif dz == 4: ready = [("bz", p, 1, 4), ("bz", p, -1, 4)]
            else: ready = [("bz", p, 1 if dz < 0 else -1, abs(dz))]
            for s in SIGNS:
                add(("bx", p, dz, s, 1), name("x", s), fb, ready)
                add(("bx", p, dz, s, 2), name("x", s), fb / 2, [("bx", p, dz, s, 1)])
    for q in (0, 1):
        kd="out" if q==0 else "back"
        fa = o["ra"][2 + q] / ROWS
        fb = 1 - fa
        def gate(c): return [("gate","rs",q)] + ([("gate2","rs",q)] if c else [])
        def done_a(dx): return [("rz", q, dx, s, 1) for s in SIGNS]
        def done_b(dz): return [("sx", q, dz, s, 1) for s in SIGNS]
        for dx in o["dxs"]:
            for s in SIGNS:
                for k in (4, 3, 2, 1):
                    add(("rz", q, dx, s, k), name("z", s), fa if k < 4 else fa / 2, (gate(dx in o.get("late_dx",())) if k == 4 else [("rz", q, dx, s, k + 1)])+[(kd,nz(s*k))])
        for dz in o["dzs"]:
            for s in SIGNS:
                add(("sx", q, dz, s, 2), name("x", s), fb / 2, gate(dz in o.get("late_dz",()))+[(kd,dz)])
                add(("sx", q, dz, s, 1), name("x", s), fb, [("sx", q, dz, s, 2)])
        for s in SIGNS:
            add(("rx", q, s, 2), name("x", s), fa / 2, done_a(2))
            add(("rx", q, s, 1), name("x", s), fa, [("rx", q, s, 2)] + done_a(s))
            add(("sz", q, s, 4), name("z", s), fb / 2, done_b(4))
            for k in (3, 2, 1):
                add(("sz", q, s, k), name("z", s), fb, [("sz", q, s, k + 1)] + done_b(s * k))
    for m in (0, 1):
        for v in (0,1):
            add(("pc", m, v), "c", o["cl"]/2, [("grad", m, v)])
        pcs=[("pc",m,0),("pc",m,1),("grad",m,2)]
        for u in (0,1):
            for s in SIGNS:
                add(("yr", m, u, s, 2), name("y", s), 0.5, pcs)
                add(("yr", m, u, s, 1), name("y", s), 1.0, [("yr", m, u, s, 2)])
        for u in (0,1):
            fin = [("yr", m, u, s, 1) for s in SIGNS]
            for s in SIGNS:
                add(("yg", m, u, s, 1), name("y", s), 1.0, fin)
                add(("yg", m, u, s, 2), name("y", s), 0.5, [("yg", m, u, s, 1)])
            add(("cg", m, u, 0), "c", 0.2, fin)
            add(("cg", m, u, -1), "c", 0.2, [("yg", m, u, 1, 1)])
            add(("cg", m, u, 1), "c", 0.2, [("yg", m, u, -1, 1)])
            add(("cg", m, u, 2), "c", 0.2, [("yg", m, u, 1, 2), ("yg", m, u, -1, 2)])
    return items
def build_chunks(o, items):
    def all_of(kinds, p): return [k for k in items if k[0] in kinds and k[1] == p]
    ag = ("ax", "az", "bz", "bx")
    chunks = [(("load",), 0.3, [("count", "ag", 0, 30)])]
    chunks += [(("pre", i), 0.56, all_of(ag, 0) + [("load",)]) for i in range(4)]
    pre = [("pre", i) for i in range(4)]
    chunks += [(("out", dz), 1.25, pre) for dz in o["dzs"]]
    agr = [("agrad", i) for i in range(4)]
    tail=[(("back",dz),1.33,agr) for dz in o["dzs"]]
    ft=[(("fterm",i),.63,agr) for i in range(4)]
    st=[(("sterm",i),.5,all_of(ag,1)+pre) for i in range(4)]
    tail[o["pf"]:o["pf"]]=ft
    ps=o["ps"]
    if ps>=0: tail[ps:ps]=st
    ag_=[(("agrad",i),.55,all_of(ag,1)+pre) for i in range(4)]
    chunks += (st if ps<0 else [])+ag_+tail
    return chunks
def build_marks(o, items):
    final = [[("rx", q, s, 1) for s in SIGNS]+ [("rz", q, 0, s, 1) for s in SIGNS]+ [("sz", q, s, 1) for s in SIGNS]+ [("sx", q, 0, s, 1) for s in SIGNS] for q in (0, 1)]
    marks = [
        (("gate", "ag", 0), []),
        (("gate", "ag", 1), [("count", "ag", 0, o["g1"])]),
        (("gate", "rs", 0), [("count", "ag", 1, o["g2"])]),
        (("gate", "rs", 1), [("count", "rs", 0, o["g3"])]),
        (("gate2", "rs", 0), [("count", "rs", 0, o.get("h",0))]),
        (("gate2", "rs", 1), [("count", "rs", 1, o.get("h",0))]),
        (("store", 0), final[0]),(("store", 1), final[1]),
    ]
    for m,n in ((0,"sterm"),(1,"fterm")):
        marks += [(("grad", m, 0), [(n,0)]),(("grad", m, 1), [(n,1)]),(("grad", m, 2), [(n,i) for i in range(4)])]
        for u in (0,1): marks.append((("own",m,u),[("yr",m,u,s,1) for s in SIGNS]))
    return marks
def build_order(o):
    items = build_items(o); chunks = build_chunks(o, items); marks = build_marks(o, items)
    UNIT,LAT=o["UNIT"],o["LAT"]
    got, counts, free = set(), {}, {}
    waiting = list(items); heap, order = [], []; now, seq = 0.0, 0
    pend={}; members={}
    for k in items: members[pair_of(k)]=members.get(pair_of(k),0)+1
    def met(need):
        if need[0] == "count": return counts.get((need[1], need[2]), 0) >= need[3]
        return need in got
    def settle():
        nonlocal now, seq
        moved = True
        while moved:
            moved = False
            for mark in list(marks):
                if all(met(n) for n in mark[1]):
                    marks.remove(mark); order.append(("mark", mark[0])); got.add(mark[0]); moved = True
            for key in list(waiting):
                link, size, deps = items[key]
                if all(d in got for d in deps):
                    waiting.remove(key); order.append(("send", key)); now += 0.03
                    start = max(now, free.get(link, 0.0))
                    free[link] = start + size * UNIT; seq += 1
                    pair=pair_of(key); pend.setdefault(pair,[]).append(free[link]+LAT)
                    if len(pend[pair])==members[pair]: heapq.heappush(heap, (max(pend[pair]), seq, pair))
                    moved = True
    settle()
    held=[]
    while heap or chunks or held:
        key=None
        for h in held:
            if all(n in got for n in recv_need(h)): key=h; held.remove(h); break
        if key is None and heap and heap[0][0] <= now:
            key = heapq.heappop(heap)[2]
            if not all(n in got for n in recv_need(key)): held.append(key); continue
        if key is not None:
            order.append(("recv", key)); got.update(k for k in items if pair_of(k)==key)
            group = GROUP.get(key[0], "ar"); counts[(group, key[1])] = counts.get((group, key[1]), 0) + members[key]
            now += COST.get(group, 0.2); settle(); continue
        if chunks and all(met(n) for n in chunks[0][2]):
            key, time, _ = chunks.pop(0); order.append(("comp", key)); got.add(key); now += time
            settle(); continue
        if not heap: return None
        now = max(now, heap[0][0])
    if waiting or marks: return None
    return list(items), order, now


KEYS, ORDER, SPAN = build_order(OPT)
PAIRS = list(dict.fromkeys(pair_of(k) for k in KEYS))
INDEX = {k: i for i, k in enumerate(PAIRS)}


def slot_index():
    a, b, y = {}, {}, {}
    na = nb = ny = 0
    for k in PAIRS:
        split = k[-1] == (4 if k[0][-1] == "z" else 2)
        n = 1 if split else 2
        if k[0] in ("rz", "rx") and k[1] == 0:
            a[(k[0],) + k[2:]] = na
            na += n
        if k[0] in ("sx", "sz") and k[1] == 0:
            b[(k[0],) + k[2:]] = nb
            nb += n
        if k[0] == "yr" and k[1:3] == (0, 0):
            y[k[-1]] = ny
            ny += n
    return a, b, y, na, nb, ny


SLOT_A, SLOT_B, SLOT_Y, NA, NB, NYS = slot_index()
SENT = {"ag": (0, 1), "rs": (0, 1), "ar": (0, 1)}
SEND = {"ag": 0, "rs": 2, "pc": 4, "yr": 4, "yg": 6, "cg": 6}


def gelu_pair(value):
    inner = gelu_scale * (value + gelu_cube * value * value * value)
    tangent = jnp.tanh(inner)
    result = 0.5 * value * (1.0 + tangent)
    slope = 0.5 * (1.0 + tangent) + 0.5 * value * (1.0 - tangent * tangent) * gelu_scale * (
        1.0 + 3.0 * gelu_cube * value * value
    )
    return result, slope


def kernel(
    tokens, grads, patv, pats, first, second,
    out_ref, back_ref, fgrad_ref, sgrad_ref,
    xb, gb, part0, part1, slot_a, slot_b, w1, w2, act, pgrad, slope_ref,
    sgr, fgr, pair, yslot, invv, invs,
    send_sem, recv_sem, local_sem,
):
    t = lax.axis_index("tensor")
    d = lax.axis_index("dp")
    x, z = lax.div(t, NZ), lax.rem(t, NZ)
    y, core = lax.div(d, 2), lax.rem(d, 2)

    def at(dx, dz):
        return lax.rem(x + (dx + NX), NX) * NZ + lax.rem(z + (dz + NZ), NZ)

    def dev_x(s):
        return {"tensor": at(s, 0)}

    def dev_z(s):
        return {"tensor": at(0, s)}

    def dev_y(s):
        return {"dp": lax.rem(y + (s + NY), NY) * 2 + core}

    partner = {"dp": y * 2 + (1 - core)}
    base = core * 4

    def yrow(dy, b=None):
        return (base if b is None else b) + lax.rem(y + (dy + NY), NY)

    barrier = pltpu.get_barrier_semaphore()
    for dev in (dev_x(1), dev_x(-1), dev_z(1), dev_z(-1), dev_y(1), dev_y(-1), partner):
        pl.semaphore_signal(barrier, inc=1, device_id=dev, device_id_type=MESH)

    local = []
    for n, (src, buf) in enumerate(((tokens, xb), (grads, gb))):
        for h in (0, 1):
            c = pltpu.make_async_copy(
                src.at[:, pl.ds(h * BLK, BLK)], buf.at[t, h], local_sem.at[2 * n + h]
            )
            c.start()
            local.append(c)
    load_w1 = pltpu.make_async_copy(first, w1.at[:, pl.ds(0, K)], local_sem.at[4])
    load_w2 = pltpu.make_async_copy(second, w2.at[:, pl.ds(0, K)], local_sem.at[5])
    load_w1.start()
    load_w2.start()

    cols = lax.broadcasted_iota(jnp.int32, (HR, BLK), 1)
    inv = jnp.full((HR, BLK), K, jnp.int32)
    for j in range(K):
        inv = jnp.where(patv[:, j : j + 1] == cols, j, inv)
    invv[...] = inv
    load_inv = pltpu.make_async_copy(invv, invs, local_sem.at[6])
    load_inv.start()
    for c in local:
        c.wait()

    pl.semaphore_wait(barrier, 7)

    gathered = (xb, gb)
    parts = (part0, part1)
    grad_of = (sgr, fgr)
    grad_out = (sgrad_ref, fgrad_ref)
    rows_a, rows_b = pl.ds(0, RA), pl.ds(RA, RB)

    def half(s):
        return 0 if s > 0 else 1

    def reduce_slot(key):
        kind, q, s, k = key[0], key[1], key[-2], key[-1]
        sub = (kind,) + key[2:-2] + (k,)
        split = k == (4 if kind[1] == "z" else 2)
        lane = 0 if split or s > 0 else 1
        if kind[0] == "r":
            return rows_a, slot_a.at[q, SLOT_A[sub] + lane], split
        return rows_b, slot_b.at[q, SLOT_B[sub] + lane], split

    def reduce_shard(key, k):
        kind, s = key[0], key[-2]
        if kind == "rz":
            return at(key[2], s * k)
        if kind == "sz":
            return at(0, s * k)
        if kind == "rx":
            return at(s * k, 0)
        return at(s * k, key[2])

    def copy_of(key):
        kind, p = key[0], key[1]
        group = GROUP.get(kind, kind)
        ss, rs = send_sem.at[SEND[group] + p], recv_sem.at[INDEX[pair_of(key)]]

        def remote(src, dst, dev):
            return pltpu.make_async_remote_copy(
                src_ref=src, dst_ref=dst, send_sem=ss, recv_sem=rs, device_id=dev, device_id_type=MESH
            )

        if group == "ag":
            s, k = key[-2], key[-1]
            rows = rows_a if kind[0] == "a" else rows_b
            if kind == "ax":
                own, dev, split = at(-s * (k - 1), 0), dev_x(s), k == 2
            elif kind == "az":
                own, dev, split = at(key[2], -s * (k - 1)), dev_z(s), k == 4
            elif kind == "bz":
                own, dev, split = at(0, -s * (k - 1)), dev_z(s), k == 4
            else:
                own, dev, split = at(-s * (k - 1), key[2]), dev_x(s), k == 2
            view = gathered[p].at[own, pl.ds(half(s), 1) if split else pl.ds(0, 2), rows, :]
            return remote(view, view, dev)
        if group == "rs":
            s, k = key[-2], key[-1]
            rows, slot, split = reduce_slot(key)
            hs = pl.ds(half(s), 1) if split else pl.ds(0, 2)
            dev = dev_z(s) if kind[1] == "z" else dev_x(s)
            return remote(parts[p].at[reduce_shard(key, k), hs, rows, :], slot.at[hs], dev)
        g, out = grad_of[p], grad_out[p]
        if kind == "pc":
            v = key[2] * 2
            return remote(g.at[pl.ds((1 - core) * 4 + v, 2)], pair.at[p, pl.ds(v, 2)], partner)
        u, s, k = key[2] * 4, key[-2], key[-1]
        if kind == "cg":
            js, dy = pl.ds(u, 4), key[3]
            src = g.at[yrow(0), js] if dy == 0 else out.at[yrow(dy), js]
            return remote(src, out.at[yrow(dy), js], partner)
        js = pl.ds(u + half(s) * 2, 2) if k == 2 else pl.ds(u, 4)
        if kind == "yr":
            slot = SLOT_Y[k] + (0 if k == 2 or s > 0 else 1)
            return remote(g.at[yrow(s * k), js], yslot.at[p, slot, js], dev_y(s))
        src = g.at[yrow(0), js] if k == 1 else out.at[yrow(-s), js]
        return remote(src, out.at[yrow(-s * (k - 1)), js], dev_y(s))

    def wait_for(view, sem, sent=False):
        c = pltpu.make_async_remote_copy(
            src_ref=view, dst_ref=view, send_sem=sem, recv_sem=sem, device_id=partner, device_id_type=MESH
        )
        if sent:
            c.wait_send()
        else:
            c.wait_recv()

    def received(key):
        kind, p = key[0], key[1]
        sem = recv_sem.at[INDEX[key]]
        group = GROUP.get(kind, kind)
        if group == "ag":
            rows = rows_a if kind[0] == "a" else rows_b
            split = key[-1] == (4 if kind[1] == "z" else 2)
            wait_for(gathered[p].at[pl.ds(0, 1 if split else 2), :, rows, :], sem)
        elif group == "rs":
            split = key[-1] == (4 if kind[1] == "z" else 2)
            signed = [key[:-1] + (s, key[-1]) for s in SIGNS]
            rows = rows_a if kind[0] == "r" else rows_b
            wait_for(parts[p].at[pl.ds(0, 1 if split else 2), :, rows, :], sem)
            places = [reduce_shard(k, key[-1] - 1) for k in signed]
            slots = [reduce_slot(k)[1] for k in signed]
            if key[-1] == 1:
                for h in (0, 1):
                    total = parts[p][places[0], h, rows, :].astype(F32)
                    total = total + slots[0][h].astype(F32) + slots[1][h].astype(F32)
                    parts[p][places[0], h, rows, :] = total.astype(BF)
                return
            for s, mine, slot in zip(SIGNS, places, slots):
                for h in (half(s),) if split else (0, 1):
                    total = parts[p][mine, h, rows, :].astype(F32) + slot[h].astype(F32)
                    parts[p][mine, h, rows, :] = total.astype(BF)
        elif kind == "pc":
            v = key[2] * 2
            g = grad_of[p]
            wait_for(pair.at[p, pl.ds(v, 2)], sem)

            @pl.loop(v, v + 2)
            def _(r):
                @pl.loop(0, K)
                def _(j):
                    total = g[base + r, j].astype(F32) + pair[p, r, j].astype(F32)
                    g[base + r, j] = total.astype(BF)
        elif kind == "yr":
            u, k = key[2] * 4, key[-1]
            g = grad_of[p]
            if k == 2:
                wait_for(yslot.at[p, SLOT_Y[2], pl.ds(u, 4)], sem)
                for s in SIGNS:
                    row = yrow(s)
                    lo = u + half(s) * 2

                    @pl.loop(lo, lo + 2)
                    def _(j):
                        total = g[row, j].astype(F32) + yslot[p, SLOT_Y[2], j].astype(F32)
                        g[row, j] = total.astype(BF)
            else:
                wait_for(yslot.at[p, pl.ds(SLOT_Y[1], 2), pl.ds(u, 4)], sem)
                row = yrow(0)

                @pl.loop(u, u + 4)
                def _(j):
                    total = g[row, j].astype(F32) + yslot[p, SLOT_Y[1], j].astype(F32)
                    total = total + yslot[p, SLOT_Y[1] + 1, j].astype(F32)
                    g[row, j] = total.astype(BF)
        elif kind == "yg":
            wait_for(grad_out[p].at[pl.ds(0, 2 if key[-1] == 1 else 1), pl.ds(key[2] * 4, 4)], sem)
        else:
            wait_for(grad_out[p].at[pl.ds(0, 4)], sem)

    def picked(buf, r):
        return jnp.concatenate([buf[lax.div(pats[r, j], 2), lax.rem(pats[r, j], 2)] for j in range(K)], axis=1)

    def whole(ref):
        return jnp.concatenate([ref[r] for r in range(HR)], axis=1)

    nt = (((1,), (1,)), ((), ()))

    def compute(key):
        kind = key[0]
        if kind == "load":
            load_w1.wait()
            load_w2.wait()
            load_inv.wait()
            for w in (w1, w2):
                for r in range(HR):
                    w[r, K] = jnp.zeros((BLK, BLK), BF)
            return
        i = key[1]
        if kind in ("out", "back"):

            @pl.loop(0, NX)
            def _(dx):
                dest = lax.rem(x + dx, NX) * NZ + lax.rem(z + (i + NZ), NZ)
                if kind == "out":
                    rhs = jnp.concatenate(
                        [
                            jnp.concatenate([w2[r, invs[r, 2 * dest + h]] for r in range(HR)], axis=0)
                            for h in (0, 1)
                        ],
                        axis=1,
                    )
                    res = jnp.dot(whole(act), rhs, preferred_element_type=F32)
                else:
                    rhs = jnp.concatenate(
                        [
                            jnp.concatenate([w1[r, invs[r, 2 * dest + h]] for r in range(HR)], axis=1)
                            for h in (0, 1)
                        ],
                        axis=0,
                    )
                    res = lax.dot_general(whole(pgrad), rhs, nt, preferred_element_type=F32)
                buf = part0 if kind == "out" else part1
                for h in (0, 1):
                    buf[dest, h] = res[:, h * BLK : (h + 1) * BLK].astype(BF)

            return

        @pl.loop(i * 2, i * 2 + 2)
        def _(n):
            r = lax.rem((1 - core) * 4 + n, HR)
            if kind == "pre":
                weights = jnp.concatenate([w1[r, j] for j in range(K)], axis=0)
                pre = jnp.dot(picked(xb, r), weights, preferred_element_type=F32)
                value, slope = gelu_pair(pre)
                act[r] = value.astype(BF)
                slope_ref[r] = slope
            elif kind == "sterm":
                res = jnp.dot(act[r].T, picked(gb, r), preferred_element_type=F32)
                for j in range(K):
                    sgr[r, j] = res[:, j * BLK : (j + 1) * BLK].astype(BF)
            elif kind == "agrad":
                weights = jnp.concatenate([w2[r, j] for j in range(K)], axis=1)
                res = lax.dot_general(picked(gb, r), weights, nt, preferred_element_type=F32)
                pgrad[r] = (res * slope_ref[r]).astype(BF)
            elif kind == "fterm":
                res = jnp.dot(pgrad[r].T, picked(xb, r), preferred_element_type=F32)
                for j in range(K):
                    fgr[r, j] = res[:, j * BLK : (j + 1) * BLK].astype(BF).T

    stores = []

    def store(src, dst):
        c = pltpu.make_async_copy(src, dst, local_sem.at[8 + len(stores)])
        c.start()
        stores.append(c)

    def marked(key):
        if key[0] == "store":
            q = key[1]
            dst = (out_ref, back_ref)[q]
            for h in (0, 1):
                store(parts[q].at[t, h], dst.at[:, pl.ds(h * BLK, BLK)])
        elif key[0] == "own":
            m, js = key[1], pl.ds(key[2] * 4, 4)
            store(grad_of[m].at[yrow(0), js], grad_out[m].at[yrow(0), js])

    for action, key in ORDER:
        if action == "send":
            copy_of(key).start()
        elif action == "recv":
            received(key)
        elif action == "comp":
            compute(key)
        else:
            marked(key)
    for p in (0, 1):
        if p in SENT["ag"]:
            wait_for(gathered[p].at[pl.ds(0, 31)], send_sem.at[SEND["ag"] + p], True)
        if p in SENT["rs"]:
            wait_for(parts[p].at[pl.ds(0, 31)], send_sem.at[SEND["rs"] + p], True)
        if p in SENT["ar"]:
            wait_for(grad_of[p].at[pl.ds(0, 7)], send_sem.at[SEND["yr"] + p], True)
            wait_for(grad_of[p].at[pl.ds(0, 7)], send_sem.at[SEND["yg"] + p], True)
    for c in stores:
        c.wait()


def finish(*refs):
    srcs, dsts, sem = refs[:4], refs[4:8], refs[8]
    copies = [pltpu.make_async_copy(src, dst, sem.at[i]) for i, (src, dst) in enumerate(zip(srcs, dsts))]
    for c in copies:
        c.start()
    for c in copies:
        c.wait()


def shards(tokens, pattern, first_blocks, second_blocks, out_grad):
    any_space = pl.BlockSpec(memory_space=pltpu.HBM)
    n = len(PAIRS)
    shapes = (
            jax.ShapeDtypeStruct(tokens.shape, BF),
            jax.ShapeDtypeStruct(tokens.shape, BF),
            jax.ShapeDtypeStruct(first_blocks.shape, BF),
            jax.ShapeDtypeStruct(second_blocks.shape, BF),
        )
    results = pl.pallas_call(
        kernel,
        out_shape=tuple(pltpu.VMEM(r.shape, BF) for r in shapes),
        in_specs=[
            any_space,
            any_space,
            pl.BlockSpec(memory_space=pltpu.VMEM),
            pl.BlockSpec(memory_space=pltpu.SMEM),
            any_space,
            any_space,
        ],
        out_specs=(pl.BlockSpec(memory_space=pltpu.VMEM),) * 4,
        scratch_shapes=[
            pltpu.VMEM((32, 2, ROWS, BLK), BF),
            pltpu.VMEM((32, 2, ROWS, BLK), BF),
            pltpu.VMEM((32, 2, ROWS, BLK), BF),
            pltpu.VMEM((32, 2, ROWS, BLK), BF),
            pltpu.VMEM((2, NA, 2, RA, BLK), BF),
            pltpu.VMEM((2, NB, 2, RB, BLK), BF),
            pltpu.VMEM((HR, K + 1, BLK, BLK), BF),
            pltpu.VMEM((HR, K + 1, BLK, BLK), BF),
            pltpu.VMEM((HR, ROWS, BLK), BF),
            pltpu.VMEM((HR, ROWS, BLK), BF),
            pltpu.VMEM((HR, ROWS, BLK), F32),
            pltpu.VMEM((HR, K, BLK, BLK), BF),
            pltpu.VMEM((HR, K, BLK, BLK), BF),
            pltpu.VMEM((2, 4, K, BLK, BLK), BF),
            pltpu.VMEM((2, NYS, K, BLK, BLK), BF),
            pltpu.VMEM((HR, BLK), jnp.int32),
            pltpu.SMEM((HR, BLK), jnp.int32),
            pltpu.SemaphoreType.DMA((8,)),
            pltpu.SemaphoreType.DMA((n,)),
            pltpu.SemaphoreType.DMA((16,)),
        ],
        compiler_params=pltpu.CompilerParams(
            collective_id=0, has_side_effects=True, vmem_limit_bytes=62500000
        ),
    )(tokens, out_grad, pattern, pattern, first_blocks, second_blocks)
    return pl.pallas_call(
        finish,
        out_shape=shapes,
        in_specs=[pl.BlockSpec(memory_space=pltpu.VMEM)] * 4,
        out_specs=(any_space,) * 4,
        scratch_shapes=[pltpu.SemaphoreType.DMA((4,))],
        compiler_params=pltpu.CompilerParams(vmem_limit_bytes=4 * 1024 * 1024),
    )(*[pltpu.with_memory_space_constraint(r, pltpu.VMEM) for r in results])


def solution(mesh):
    placed = (
        P("dp", "tensor"),
        P("tensor", None),
        P("tensor", None, None, None),
        P("tensor", None, None, None),
        P("dp", "tensor"),
    )
    return jax.shard_map(
        shards,
        mesh=mesh,
        in_specs=placed,
        out_specs=(
            P("dp", "tensor"),
            P("dp", "tensor"),
            P("tensor", None, None, None),
            P("tensor", None, None, None),
        ),
        check_vma=False,
    )
```

```python
import heapq

import jax
import jax.numpy as jnp
from jax import lax
from jax.experimental import pallas as pl
from jax.experimental.pallas import tpu as pltpu
from jax.sharding import PartitionSpec as P

MESH = pl.DeviceIdType.MESH
BF = jnp.bfloat16
F32 = jnp.float32

gelu_scale = 0.7978845608028654
gelu_cube = 0.044715

NX, NZ, NY = 4, 8, 4
ROWS, BLK, HR, K = 256, 128, 8, 8
SIGNS = (1, -1)


OPT = dict(
    ra=(96, 112, 112, 96),
    UNIT=2.75,
    LAT=2.5,
    TH=1.5,
    PH=30,
    y=0.93,
    g1=8,
    g2=52,
    g3=60,
    dzs=(4, 3, -3, 2, -2, 1, -1, 0),
    dxs=(2, 1, -1, 0),
    pf=0,
    ps=-1,
    cl=0.8,
    h=4,
    late_dx=(0,),
    late_dz=(0, 1, -1),
)
SPLIT = OPT["ra"]
RA, RB = max(SPLIT), ROWS - min(SPLIT)
GROUP = {k: "ag" for k in ("ax", "az", "bz", "bx")} | {k: "rs" for k in ("rz", "rx", "sx", "sz")}
COST = {"ag": 0.03, "rs": 0.22}


def name(axis, s):
    return axis + ("+" if s > 0 else "-")


DZ=(4,3,-3,2,-2,1,-1,0)
def nz(dz): return 4 if dz==-4 else dz
def pair_of(key):
    if key[0]=="pc": return key
    if key[0]=="cg": return key[:2]
    return key[:-2]+key[-1:]
def recv_need(key):
    kind="out" if key[1]==0 else "back"
    if key[0] in ("rz","sz"): return [(kind, nz(c*(key[-1]-1))) for c in SIGNS]
    if key[0]=="rx": return [(kind,0)]
    if key[0]=="sx": return [(kind,key[2])]
    if key[0]=="pc": return [("grad",key[1],2)]
    return []
def build_items(o):
    items={}
    def add(key, link, size, deps): items[key]=(link,size,tuple(deps))
    for p in (0, 1):
        gate = [("gate", "ag", p)]
        fa = o["ra"][p] / ROWS
        fb = 1 - fa
        for s in SIGNS:
            add(("bz", p, s, 1), name("z", s), fb, gate)
            add(("ax", p, s, 1), name("x", s), fa, gate)
        for s in SIGNS:
            add(("az", p, 0, s, 1), name("z", s), fa, gate)
            add(("bx", p, 0, s, 1), name("x", s), fb, gate)
        for s in SIGNS:
            add(("ax", p, s, 2), name("x", s), fa / 2, [("ax", p, s, 1)])
            for k in (2, 3, 4):
                add(("bz", p, s, k), name("z", s), fb if k < 4 else fb / 2, [("bz", p, s, k - 1)])
        for dx, ready in ((0, gate),(-1, [("ax", p, 1, 1)]),(1, [("ax", p, -1, 1)]),(2, [("ax", p, 1, 2), ("ax", p, -1, 2)])):
            for s in SIGNS:
                for k in (1, 2, 3, 4):
                    add(("az", p, dx, s, k), name("z", s), fa if k < 4 else fa / 2, ready if k == 1 else [("az", p, dx, s, k - 1)])
        for dz in (0, -1, 1, -2, 2, -3, 3, 4):
            if dz == 0: ready = gate
            elif dz == 4: ready = [("bz", p, 1, 4), ("bz", p, -1, 4)]
            else: ready = [("bz", p, 1 if dz < 0 else -1, abs(dz))]
            for s in SIGNS:
                add(("bx", p, dz, s, 1), name("x", s), fb, ready)
                add(("bx", p, dz, s, 2), name("x", s), fb / 2, [("bx", p, dz, s, 1)])
    for q in (0, 1):
        kd="out" if q==0 else "back"
        fa = o["ra"][2 + q] / ROWS
        fb = 1 - fa
        def gate(c): return [("gate","rs",q)] + ([("gate2","rs",q)] if c else [])
        def done_a(dx): return [("rz", q, dx, s, 1) for s in SIGNS]
        def done_b(dz): return [("sx", q, dz, s, 1) for s in SIGNS]
        for dx in o["dxs"]:
            for s in SIGNS:
                for k in (4, 3, 2, 1):
                    add(("rz", q, dx, s, k), name("z", s), fa if k < 4 else fa / 2, (gate(dx in o.get("late_dx",())) if k == 4 else [("rz", q, dx, s, k + 1)])+[(kd,nz(s*k))])
        for dz in o["dzs"]:
            for s in SIGNS:
                add(("sx", q, dz, s, 2), name("x", s), fb / 2, gate(dz in o.get("late_dz",()))+[(kd,dz)])
                add(("sx", q, dz, s, 1), name("x", s), fb, [("sx", q, dz, s, 2)])
        for s in SIGNS:
            add(("rx", q, s, 2), name("x", s), fa / 2, done_a(2))
            add(("rx", q, s, 1), name("x", s), fa, [("rx", q, s, 2)] + done_a(s))
            add(("sz", q, s, 4), name("z", s), fb / 2, done_b(4))
            for k in (3, 2, 1):
                add(("sz", q, s, k), name("z", s), fb, [("sz", q, s, k + 1)] + done_b(s * k))
    for m in (0, 1):
        for v in (0,1):
            add(("pc", m, v), "c", o["cl"]/2, [("grad", m, v)])
        pcs=[("pc",m,0),("pc",m,1),("grad",m,2)]
        for u in (0,1):
            for s in SIGNS:
                add(("yr", m, u, s, 2), name("y", s), 0.5, pcs)
                add(("yr", m, u, s, 1), name("y", s), 1.0, [("yr", m, u, s, 2)])
        for u in (0,1):
            fin = [("yr", m, u, s, 1) for s in SIGNS]
            for s in SIGNS:
                add(("yg", m, u, s, 1), name("y", s), 1.0, fin)
                add(("yg", m, u, s, 2), name("y", s), 0.5, [("yg", m, u, s, 1)])
            add(("cg", m, u, 0), "c", 0.2, fin)
            add(("cg", m, u, -1), "c", 0.2, [("yg", m, u, 1, 1)])
            add(("cg", m, u, 1), "c", 0.2, [("yg", m, u, -1, 1)])
            add(("cg", m, u, 2), "c", 0.2, [("yg", m, u, 1, 2), ("yg", m, u, -1, 2)])
    return items
def build_chunks(o, items):
    def all_of(kinds, p): return [k for k in items if k[0] in kinds and k[1] == p]
    ag = ("ax", "az", "bz", "bx")
    chunks = [(("load",), 0.3, [("count", "ag", 0, 30)])]
    chunks += [(("pre", i), 0.56, all_of(ag, 0) + [("load",)]) for i in range(4)]
    pre = [("pre", i) for i in range(4)]
    chunks += [(("out", dz), 1.25, pre) for dz in o["dzs"]]
    agr = [("agrad", i) for i in range(4)]
    tail=[(("back",dz),1.33,agr) for dz in o["dzs"]]
    ft=[(("fterm",i),.63,agr) for i in range(4)]
    st=[(("sterm",i),.5,all_of(ag,1)+pre) for i in range(4)]
    tail[o["pf"]:o["pf"]]=ft
    ps=o["ps"]
    if ps>=0: tail[ps:ps]=st
    ag_=[(("agrad",i),.55,all_of(ag,1)+pre) for i in range(4)]
    chunks += (st if ps<0 else [])+ag_+tail
    return chunks
def build_marks(o, items):
    final = [[("rx", q, s, 1) for s in SIGNS]+ [("rz", q, 0, s, 1) for s in SIGNS]+ [("sz", q, s, 1) for s in SIGNS]+ [("sx", q, 0, s, 1) for s in SIGNS] for q in (0, 1)]
    marks = [
        (("gate", "ag", 0), []),
        (("gate", "ag", 1), [("count", "ag", 0, o["g1"])]),
        (("gate", "rs", 0), [("count", "ag", 1, o["g2"])]),
        (("gate", "rs", 1), [("count", "rs", 0, o["g3"])]),
        (("gate2", "rs", 0), [("count", "rs", 0, o.get("h",0))]),
        (("gate2", "rs", 1), [("count", "rs", 1, o.get("h",0))]),
        (("store", 0), final[0]),(("store", 1), final[1]),
    ]
    for m,n in ((0,"sterm"),(1,"fterm")):
        marks += [(("grad", m, 0), [(n,0)]),(("grad", m, 1), [(n,1)]),(("grad", m, 2), [(n,i) for i in range(4)])]
        for u in (0,1): marks.append((("own",m,u),[("yr",m,u,s,1) for s in SIGNS]))
    return marks
def ranks(o, items):
    after={}
    for k,(_,_,deps) in items.items():
        for d in deps: after.setdefault(d,[]).append(k)
    left={}
    def way(k):
        if k not in left: left[k]=items[k][1]*o["UNIT"]+o["LAT"]+max([way(n) for n in after.get(k,[])]+[0.0])
        return left[k]
    def phase(k):
        g=GROUP.get(k[0],"ar")
        return k[1] if g=="ag" else 2+k[1] if g=="rs" else k[1]
    return {k:(phase(k)*o["PH"]-way(k),i) for i,k in enumerate(items)}
def build_order(o):
    items = build_items(o); chunks = build_chunks(o, items); marks = build_marks(o, items)
    UNIT,LAT=o["UNIT"],o["LAT"]
    got, counts, free = set(), {}, {}
    waiting = list(items); heap, order = [], []; now, seq = 0.0, 0
    pend={}; members={}; ready=[]; rank=ranks(o, items)
    for k in items: members[pair_of(k)]=members.get(pair_of(k),0)+1
    def met(need):
        if need[0] == "count": return counts.get((need[1], need[2]), 0) >= need[3]
        return need in got
    def settle():
        nonlocal now, seq
        moved = True
        while moved:
            moved = False
            for mark in list(marks):
                if all(met(n) for n in mark[1]):
                    marks.remove(mark); order.append(("mark", mark[0])); got.add(mark[0]); moved = True
            for key in list(waiting):
                if all(d in got for d in items[key][2]):
                    waiting.remove(key); ready.append(key)
            ready.sort(key=lambda k: rank[k])
            for key in list(ready):
                link, size, _ = items[key]
                if free.get(link, 0.0) - now < o["TH"]:
                    ready.remove(key); order.append(("send", key)); now += 0.03
                    start = max(now, free.get(link, 0.0))
                    free[link] = start + size * UNIT * o.get(link[0], 1.0); seq += 1
                    pair=pair_of(key); pend.setdefault(pair,[]).append(free[link]+LAT)
                    if len(pend[pair])==members[pair]: heapq.heappush(heap, (max(pend[pair]), seq, pair))
                    moved = True
    settle()
    held=[]
    while heap or chunks or held:
        key=None
        for h in held:
            if all(n in got for n in recv_need(h)): key=h; held.remove(h); break
        if key is None and heap and heap[0][0] <= now:
            key = heapq.heappop(heap)[2]
            if not all(n in got for n in recv_need(key)): held.append(key); continue
        if key is not None:
            order.append(("recv", key)); got.update(k for k in items if pair_of(k)==key)
            group = GROUP.get(key[0], "ar"); counts[(group, key[1])] = counts.get((group, key[1]), 0) + members[key]
            now += COST.get(group, 0.2); settle(); continue
        if chunks and all(met(n) for n in chunks[0][2]):
            key, time, _ = chunks.pop(0); order.append(("comp", key)); got.add(key); now += time
            settle(); continue
        if not heap: return None
        now = max(now, heap[0][0])
    if waiting or marks or ready: return None
    return list(items), order, now


KEYS, ORDER, SPAN = build_order(OPT)
PAIRS = list(dict.fromkeys(pair_of(k) for k in KEYS))
INDEX = {k: i for i, k in enumerate(PAIRS)}


def slot_index():
    a, b, y = {}, {}, {}
    na = nb = ny = 0
    for k in PAIRS:
        split = k[-1] == (4 if k[0][-1] == "z" else 2)
        n = 1 if split else 2
        if k[0] in ("rz", "rx") and k[1] == 0:
            a[(k[0],) + k[2:]] = na
            na += n
        if k[0] in ("sx", "sz") and k[1] == 0:
            b[(k[0],) + k[2:]] = nb
            nb += n
        if k[0] == "yr" and k[1:3] == (0, 0):
            y[k[-1]] = ny
            ny += n
    return a, b, y, na, nb, ny


SLOT_A, SLOT_B, SLOT_Y, NA, NB, NYS = slot_index()
SENT = {"ag": (0, 1), "rs": (0, 1), "ar": (0, 1)}
SEND = {"ag": 0, "rs": 2, "pc": 4, "yr": 4, "yg": 6, "cg": 6}


def gelu_pair(value):
    inner = gelu_scale * (value + gelu_cube * value * value * value)
    tangent = jnp.tanh(inner)
    result = 0.5 * value * (1.0 + tangent)
    slope = 0.5 * (1.0 + tangent) + 0.5 * value * (1.0 - tangent * tangent) * gelu_scale * (
        1.0 + 3.0 * gelu_cube * value * value
    )
    return result, slope


def kernel(
    tokens, grads, patv, pats, first, second,
    out_ref, back_ref, fgrad_ref, sgrad_ref,
    xb, gb, part0, part1, slot_a, slot_b, w1, w2, act, pgrad, slope_ref,
    sgr, fgr, pair, yslot, invv, invs,
    send_sem, recv_sem, local_sem,
):
    t = lax.axis_index("tensor")
    d = lax.axis_index("dp")
    x, z = lax.div(t, NZ), lax.rem(t, NZ)
    y, core = lax.div(d, 2), lax.rem(d, 2)

    def at(dx, dz):
        return lax.rem(x + (dx + NX), NX) * NZ + lax.rem(z + (dz + NZ), NZ)

    def dev_x(s):
        return {"tensor": at(s, 0)}

    def dev_z(s):
        return {"tensor": at(0, s)}

    def dev_y(s):
        return {"dp": lax.rem(y + (s + NY), NY) * 2 + core}

    partner = {"dp": y * 2 + (1 - core)}
    base = core * 4

    def yrow(dy, b=None):
        return (base if b is None else b) + lax.rem(y + (dy + NY), NY)

    barrier = pltpu.get_barrier_semaphore()
    for dev in (dev_x(1), dev_x(-1), dev_z(1), dev_z(-1), dev_y(1), dev_y(-1), partner):
        pl.semaphore_signal(barrier, inc=1, device_id=dev, device_id_type=MESH)

    local = []
    for n, (src, buf) in enumerate(((tokens, xb), (grads, gb))):
        for h in (0, 1):
            c = pltpu.make_async_copy(
                src.at[:, pl.ds(h * BLK, BLK)], buf.at[t, h], local_sem.at[2 * n + h]
            )
            c.start()
            local.append(c)
    load_w1 = pltpu.make_async_copy(first, w1.at[:, pl.ds(0, K)], local_sem.at[4])
    load_w2 = pltpu.make_async_copy(second, w2.at[:, pl.ds(0, K)], local_sem.at[5])
    load_w1.start()
    load_w2.start()

    load_inv = pltpu.make_async_copy(invv, invs, local_sem.at[6])
    for c in local[:2]:
        c.wait()

    pl.semaphore_wait(barrier, 7)

    gathered = (xb, gb)
    parts = (part0, part1)
    grad_of = (sgr, fgr)
    grad_out = (sgrad_ref, fgrad_ref)

    def rows_of(key):
        n = SPLIT[key[1] + (0 if GROUP[key[0]] == "ag" else 2)]
        return (pl.ds(0, n), n) if key[0][0] in "ar" else (pl.ds(n, ROWS - n), ROWS - n)

    def half(s):
        return 0 if s > 0 else 1

    def reduce_slot(key):
        rows, n = rows_of(key)
        kind, q, s, k = key[0], key[1], key[-2], key[-1]
        sub = (kind,) + key[2:-2] + (k,)
        split = k == (4 if kind[1] == "z" else 2)
        lane = 0 if split or s > 0 else 1
        if kind[0] == "r":
            return rows, slot_a.at[q, SLOT_A[sub] + lane, :, pl.ds(0, n), :], split
        return rows, slot_b.at[q, SLOT_B[sub] + lane, :, pl.ds(0, n), :], split

    def reduce_shard(key, k):
        kind, s = key[0], key[-2]
        if kind == "rz":
            return at(key[2], s * k)
        if kind == "sz":
            return at(0, s * k)
        if kind == "rx":
            return at(s * k, 0)
        return at(s * k, key[2])

    def copy_of(key):
        kind, p = key[0], key[1]
        group = GROUP.get(kind, kind)
        ss, rs = send_sem.at[SEND[group] + p], recv_sem.at[INDEX[pair_of(key)]]

        def remote(src, dst, dev):
            return pltpu.make_async_remote_copy(
                src_ref=src, dst_ref=dst, send_sem=ss, recv_sem=rs, device_id=dev, device_id_type=MESH
            )

        if group == "ag":
            s, k = key[-2], key[-1]
            rows = rows_of(key)[0]
            if kind == "ax":
                own, dev, split = at(-s * (k - 1), 0), dev_x(s), k == 2
            elif kind == "az":
                own, dev, split = at(key[2], -s * (k - 1)), dev_z(s), k == 4
            elif kind == "bz":
                own, dev, split = at(0, -s * (k - 1)), dev_z(s), k == 4
            else:
                own, dev, split = at(-s * (k - 1), key[2]), dev_x(s), k == 2
            view = gathered[p].at[own, pl.ds(half(s), 1) if split else pl.ds(0, 2), rows, :]
            return remote(view, view, dev)
        if group == "rs":
            s, k = key[-2], key[-1]
            rows, slot, split = reduce_slot(key)
            hs = pl.ds(half(s), 1) if split else pl.ds(0, 2)
            dev = dev_z(s) if kind[1] == "z" else dev_x(s)
            return remote(parts[p].at[reduce_shard(key, k), hs, rows, :], slot.at[hs], dev)
        g, out = grad_of[p], grad_out[p]
        if kind == "pc":
            v = key[2] * 2
            return remote(g.at[pl.ds((1 - core) * 4 + v, 2)], pair.at[p, pl.ds(v, 2)], partner)
        u, s, k = key[2] * 4, key[-2], key[-1]
        if kind == "cg":
            js, dy = pl.ds(u, 4), key[3]
            src = g.at[yrow(0), js] if dy == 0 else out.at[yrow(dy), js]
            return remote(src, out.at[yrow(dy), js], partner)
        js = pl.ds(u + half(s) * 2, 2) if k == 2 else pl.ds(u, 4)
        if kind == "yr":
            slot = SLOT_Y[k] + (0 if k == 2 or s > 0 else 1)
            return remote(g.at[yrow(s * k), js], yslot.at[p, slot, js], dev_y(s))
        src = g.at[yrow(0), js] if k == 1 else out.at[yrow(-s), js]
        return remote(src, out.at[yrow(-s * (k - 1)), js], dev_y(s))

    def wait_for(view, sem, sent=False):
        c = pltpu.make_async_remote_copy(
            src_ref=view, dst_ref=view, send_sem=sem, recv_sem=sem, device_id=partner, device_id_type=MESH
        )
        if sent:
            c.wait_send()
        else:
            c.wait_recv()

    def received(key):
        kind, p = key[0], key[1]
        sem = recv_sem.at[INDEX[key]]
        group = GROUP.get(kind, kind)
        if group == "ag":
            rows = rows_of(key)[0]
            split = key[-1] == (4 if kind[1] == "z" else 2)
            wait_for(gathered[p].at[pl.ds(0, 1 if split else 2), :, rows, :], sem)
        elif group == "rs":
            split = key[-1] == (4 if kind[1] == "z" else 2)
            signed = [key[:-1] + (s, key[-1]) for s in SIGNS]
            rows = rows_of(key)[0]
            wait_for(parts[p].at[pl.ds(0, 1 if split else 2), :, rows, :], sem)
            places = [reduce_shard(k, key[-1] - 1) for k in signed]
            slots = [reduce_slot(k)[1] for k in signed]
            if key[-1] == 1:
                for h in (0, 1):
                    total = parts[p][places[0], h, rows, :].astype(F32)
                    total = total + slots[0][h].astype(F32) + slots[1][h].astype(F32)
                    parts[p][places[0], h, rows, :] = total.astype(BF)
                return
            for s, mine, slot in zip(SIGNS, places, slots):
                for h in (half(s),) if split else (0, 1):
                    total = parts[p][mine, h, rows, :].astype(F32) + slot[h].astype(F32)
                    parts[p][mine, h, rows, :] = total.astype(BF)
        elif kind == "pc":
            v = key[2] * 2
            g = grad_of[p]
            wait_for(pair.at[p, pl.ds(v, 2)], sem)

            @pl.loop(v, v + 2)
            def _(r):
                @pl.loop(0, K)
                def _(j):
                    total = g[base + r, j].astype(F32) + pair[p, r, j].astype(F32)
                    g[base + r, j] = total.astype(BF)
        elif kind == "yr":
            u, k = key[2] * 4, key[-1]
            g = grad_of[p]
            if k == 2:
                wait_for(yslot.at[p, SLOT_Y[2], pl.ds(u, 4)], sem)
                for s in SIGNS:
                    row = yrow(s)
                    lo = u + half(s) * 2

                    @pl.loop(lo, lo + 2)
                    def _(j):
                        total = g[row, j].astype(F32) + yslot[p, SLOT_Y[2], j].astype(F32)
                        g[row, j] = total.astype(BF)
            else:
                wait_for(yslot.at[p, pl.ds(SLOT_Y[1], 2), pl.ds(u, 4)], sem)
                row = yrow(0)

                @pl.loop(u, u + 4)
                def _(j):
                    total = g[row, j].astype(F32) + yslot[p, SLOT_Y[1], j].astype(F32)
                    total = total + yslot[p, SLOT_Y[1] + 1, j].astype(F32)
                    g[row, j] = total.astype(BF)
        elif kind == "yg":
            wait_for(grad_out[p].at[pl.ds(0, 2 if key[-1] == 1 else 1), pl.ds(key[2] * 4, 4)], sem)
        else:
            wait_for(grad_out[p].at[pl.ds(0, 4)], sem)

    def picked(buf, r):
        return jnp.concatenate([buf[lax.div(pats[r, j], 2), lax.rem(pats[r, j], 2)] for j in range(K)], axis=1)

    def whole(ref):
        return jnp.concatenate([ref[r] for r in range(HR)], axis=1)

    nt = (((1,), (1,)), ((), ()))

    def compute(key):
        kind = key[0]
        if kind == "load":
            cols = lax.broadcasted_iota(jnp.int32, (HR, BLK), 1)
            inv = jnp.full((HR, BLK), K, jnp.int32)
            for j in range(K):
                inv = jnp.where(patv[:, j : j + 1] == cols, j, inv)
            invv[...] = inv
            load_inv.start()
            load_w1.wait()
            load_w2.wait()
            load_inv.wait()
            for w in (w1, w2):
                for r in range(HR):
                    w[r, K] = jnp.zeros((BLK, BLK), BF)
            return
        i = key[1]
        if kind in ("out", "back"):

            @pl.loop(0, NX)
            def _(dx):
                dest = lax.rem(x + dx, NX) * NZ + lax.rem(z + (i + NZ), NZ)
                if kind == "out":
                    rhs = jnp.concatenate(
                        [
                            jnp.concatenate([w2[r, invs[r, 2 * dest + h]] for r in range(HR)], axis=0)
                            for h in (0, 1)
                        ],
                        axis=1,
                    )
                    res = jnp.dot(whole(act), rhs, preferred_element_type=F32)
                else:
                    rhs = jnp.concatenate(
                        [
                            jnp.concatenate([w1[r, invs[r, 2 * dest + h]] for r in range(HR)], axis=1)
                            for h in (0, 1)
                        ],
                        axis=0,
                    )
                    res = lax.dot_general(whole(pgrad), rhs, nt, preferred_element_type=F32)
                buf = part0 if kind == "out" else part1
                for h in (0, 1):
                    buf[dest, h] = res[:, h * BLK : (h + 1) * BLK].astype(BF)

            return

        @pl.loop(i * 2, i * 2 + 2)
        def _(n):
            r = lax.rem((1 - core) * 4 + n, HR)
            if kind == "pre":
                weights = jnp.concatenate([w1[r, j] for j in range(K)], axis=0)
                pre = jnp.dot(picked(xb, r), weights, preferred_element_type=F32)
                value, slope = gelu_pair(pre)
                act[r] = value.astype(BF)
                slope_ref[r] = slope
            elif kind == "sterm":
                res = jnp.dot(act[r].T, picked(gb, r), preferred_element_type=F32)
                for j in range(K):
                    sgr[r, j] = res[:, j * BLK : (j + 1) * BLK].astype(BF)
            elif kind == "agrad":
                weights = jnp.concatenate([w2[r, j] for j in range(K)], axis=1)
                res = lax.dot_general(picked(gb, r), weights, nt, preferred_element_type=F32)
                pgrad[r] = (res * slope_ref[r]).astype(BF)
            elif kind == "fterm":
                res = jnp.dot(pgrad[r].T, picked(xb, r), preferred_element_type=F32)
                for j in range(K):
                    fgr[r, j] = res[:, j * BLK : (j + 1) * BLK].astype(BF).T

    stores = []

    def store(src, dst):
        c = pltpu.make_async_copy(src, dst, local_sem.at[8 + len(stores)])
        c.start()
        stores.append(c)

    def marked(key):
        if key == ("gate", "ag", 1):
            for c in local[2:]:
                c.wait()
        if key[0] == "store":
            q = key[1]
            dst = (out_ref, back_ref)[q]
            for h in (0, 1):
                store(parts[q].at[t, h], dst.at[:, pl.ds(h * BLK, BLK)])
        elif key[0] == "own":
            m, js = key[1], pl.ds(key[2] * 4, 4)
            store(grad_of[m].at[yrow(0), js], grad_out[m].at[yrow(0), js])

    for action, key in ORDER:
        if action == "send":
            copy_of(key).start()
        elif action == "recv":
            received(key)
        elif action == "comp":
            compute(key)
        else:
            marked(key)
    for p in (0, 1):
        if p in SENT["ag"]:
            wait_for(gathered[p].at[pl.ds(0, 31)], send_sem.at[SEND["ag"] + p], True)
        if p in SENT["rs"]:
            wait_for(parts[p].at[pl.ds(0, 31)], send_sem.at[SEND["rs"] + p], True)
        if p in SENT["ar"]:
            wait_for(grad_of[p].at[pl.ds(0, 7)], send_sem.at[SEND["yr"] + p], True)
            wait_for(grad_of[p].at[pl.ds(0, 7)], send_sem.at[SEND["yg"] + p], True)
    for c in stores:
        c.wait()


def finish(*refs):
    srcs, dsts, sem = refs[:4], refs[4:8], refs[8]
    copies = [pltpu.make_async_copy(src, dst, sem.at[i]) for i, (src, dst) in enumerate(zip(srcs, dsts))]
    for c in copies:
        c.start()
    for c in copies:
        c.wait()


def shards(tokens, pattern, first_blocks, second_blocks, out_grad):
    any_space = pl.BlockSpec(memory_space=pltpu.HBM)
    n = len(PAIRS)
    shapes = (
            jax.ShapeDtypeStruct(tokens.shape, BF),
            jax.ShapeDtypeStruct(tokens.shape, BF),
            jax.ShapeDtypeStruct(first_blocks.shape, BF),
            jax.ShapeDtypeStruct(second_blocks.shape, BF),
        )
    results = pl.pallas_call(
        kernel,
        out_shape=tuple(pltpu.VMEM(r.shape, BF) for r in shapes),
        in_specs=[
            any_space,
            any_space,
            pl.BlockSpec(memory_space=pltpu.VMEM),
            pl.BlockSpec(memory_space=pltpu.SMEM),
            any_space,
            any_space,
        ],
        out_specs=(pl.BlockSpec(memory_space=pltpu.VMEM),) * 4,
        scratch_shapes=[
            pltpu.VMEM((32, 2, ROWS, BLK), BF),
            pltpu.VMEM((32, 2, ROWS, BLK), BF),
            pltpu.VMEM((32, 2, ROWS, BLK), BF),
            pltpu.VMEM((32, 2, ROWS, BLK), BF),
            pltpu.VMEM((2, NA, 2, RA, BLK), BF),
            pltpu.VMEM((2, NB, 2, RB, BLK), BF),
            pltpu.VMEM((HR, K + 1, BLK, BLK), BF),
            pltpu.VMEM((HR, K + 1, BLK, BLK), BF),
            pltpu.VMEM((HR, ROWS, BLK), BF),
            pltpu.VMEM((HR, ROWS, BLK), BF),
            pltpu.VMEM((HR, ROWS, BLK), F32),
            pltpu.VMEM((HR, K, BLK, BLK), BF),
            pltpu.VMEM((HR, K, BLK, BLK), BF),
            pltpu.VMEM((2, 4, K, BLK, BLK), BF),
            pltpu.VMEM((2, NYS, K, BLK, BLK), BF),
            pltpu.VMEM((HR, BLK), jnp.int32),
            pltpu.SMEM((HR, BLK), jnp.int32),
            pltpu.SemaphoreType.DMA((8,)),
            pltpu.SemaphoreType.DMA((n,)),
            pltpu.SemaphoreType.DMA((16,)),
        ],
        compiler_params=pltpu.CompilerParams(
            collective_id=0, has_side_effects=True, vmem_limit_bytes=62500000
        ),
    )(tokens, out_grad, pattern, pattern, first_blocks, second_blocks)
    return pl.pallas_call(
        finish,
        out_shape=shapes,
        in_specs=[pl.BlockSpec(memory_space=pltpu.VMEM)] * 4,
        out_specs=(any_space,) * 4,
        scratch_shapes=[pltpu.SemaphoreType.DMA((4,))],
        compiler_params=pltpu.CompilerParams(vmem_limit_bytes=4 * 1024 * 1024),
    )(*[pltpu.with_memory_space_constraint(r, pltpu.VMEM) for r in results])


def solution(mesh):
    placed = (
        P("dp", "tensor"),
        P("tensor", None),
        P("tensor", None, None, None),
        P("tensor", None, None, None),
        P("dp", "tensor"),
    )
    return jax.shard_map(
        shards,
        mesh=mesh,
        in_specs=placed,
        out_specs=(
            P("dp", "tensor"),
            P("dp", "tensor"),
            P("tensor", None, None, None),
            P("tensor", None, None, None),
        ),
        check_vma=False,
    )
```

```python
import heapq
import random

import jax
import jax.numpy as jnp
from jax import lax
from jax.experimental import pallas as pl
from jax.experimental.pallas import tpu as pltpu
from jax.sharding import PartitionSpec as P

MESH = pl.DeviceIdType.MESH
BF = jnp.bfloat16
F32 = jnp.float32

gelu_scale = 0.7978845608028654
gelu_cube = 0.044715

NX, NZ, NY = 4, 8, 4
ROWS, BLK, HR, K = 256, 128, 8, 8
SIGNS = (1, -1)


OPT = dict(
    ra=(80, 112, 112, 96),
    UNIT=2.75,
    LAT=2.5,
    TH=1.5,
    PH=20,
    np=2,
    seed=2803,
    amp=0,
    y=0.93,
    g1=8,
    g2=56,
    g3=40,
    dzs=(4, 3, -3, 2, -2, 1, -1, 0),
    dxs=(2, 1, -1, 0),
    pf=0,
    ps=-1,
    cl=0.8,
    h=4,
    late_dx=(0,),
    late_dz=(0, 1, -1, 2, -2),
)
SPLIT = OPT["ra"]
RA, RB = max(SPLIT), ROWS - min(SPLIT)
GROUP = {k: "ag" for k in ("ax", "az", "bz", "bx")} | {k: "rs" for k in ("rz", "rx", "sx", "sz")}
COST = {"ag": 0.03, "rs": 0.16}


def name(axis, s):
    return axis + ("+" if s > 0 else "-")


DZ=(4,3,-3,2,-2,1,-1,0)
def nz(dz): return 4 if dz==-4 else dz
def pair_of(key):
    if key[0]=="pc": return key
    if key[0]=="cg": return key[:2]
    return key[:-2]+key[-1:]
def recv_need(key):
    kind="out" if key[1]==0 else "back"
    if key[0] in ("rz","sz"): return [(kind, nz(c*(key[-1]-1))) for c in SIGNS]
    if key[0]=="rx": return [(kind,0)]
    if key[0]=="sx": return [(kind,key[2])]
    if key[0]=="pc": return [("grad",key[1],2)]
    return []
def build_items(o):
    items={}
    def add(key, link, size, deps): items[key]=(link,size,tuple(deps))
    for p in (0, 1):
        gate = [("gate", "ag", p)]
        fa = o["ra"][p] / ROWS
        fb = 1 - fa
        for s in SIGNS:
            add(("bz", p, s, 1), name("z", s), fb, gate)
            add(("ax", p, s, 1), name("x", s), fa, gate)
        for s in SIGNS:
            add(("az", p, 0, s, 1), name("z", s), fa, gate)
            add(("bx", p, 0, s, 1), name("x", s), fb, gate)
        for s in SIGNS:
            add(("ax", p, s, 2), name("x", s), fa / 2, [("ax", p, s, 1)])
            for k in (2, 3, 4):
                add(("bz", p, s, k), name("z", s), fb if k < 4 else fb / 2, [("bz", p, s, k - 1)])
        for dx, ready in ((0, gate),(-1, [("ax", p, 1, 1)]),(1, [("ax", p, -1, 1)]),(2, [("ax", p, 1, 2), ("ax", p, -1, 2)])):
            for s in SIGNS:
                for k in (1, 2, 3, 4):
                    add(("az", p, dx, s, k), name("z", s), fa if k < 4 else fa / 2, ready if k == 1 else [("az", p, dx, s, k - 1)])
        for dz in (0, -1, 1, -2, 2, -3, 3, 4):
            if dz == 0: ready = gate
            elif dz == 4: ready = [("bz", p, 1, 4), ("bz", p, -1, 4)]
            else: ready = [("bz", p, 1 if dz < 0 else -1, abs(dz))]
            for s in SIGNS:
                add(("bx", p, dz, s, 1), name("x", s), fb, ready)
                add(("bx", p, dz, s, 2), name("x", s), fb / 2, [("bx", p, dz, s, 1)])
    for q in (0, 1):
        kd="out" if q==0 else "back"
        fa = o["ra"][2 + q] / ROWS
        fb = 1 - fa
        def gate(c): return [("gate","rs",q)] + ([("gate2","rs",q)] if c else [])
        def done_a(dx): return [("rz", q, dx, s, 1) for s in SIGNS]
        def done_b(dz): return [("sx", q, dz, s, 1) for s in SIGNS]
        for dx in o["dxs"]:
            for s in SIGNS:
                for k in (4, 3, 2, 1):
                    add(("rz", q, dx, s, k), name("z", s), fa if k < 4 else fa / 2, (gate(dx in o.get("late_dx",())) if k == 4 else [("rz", q, dx, s, k + 1)])+[(kd,nz(s*k))])
        for dz in o["dzs"]:
            for s in SIGNS:
                add(("sx", q, dz, s, 2), name("x", s), fb / 2, gate(dz in o.get("late_dz",()))+[(kd,dz)])
                add(("sx", q, dz, s, 1), name("x", s), fb, [("sx", q, dz, s, 2)])
        for s in SIGNS:
            add(("rx", q, s, 2), name("x", s), fa / 2, done_a(2))
            add(("rx", q, s, 1), name("x", s), fa, [("rx", q, s, 2)] + done_a(s))
            add(("sz", q, s, 4), name("z", s), fb / 2, done_b(4))
            for k in (3, 2, 1):
                add(("sz", q, s, k), name("z", s), fb, [("sz", q, s, k + 1)] + done_b(s * k))
    for m in (0, 1):
        for v in (0,1):
            add(("pc", m, v), "c", o["cl"]/2, [("grad", m, v)])
        pcs=[("pc",m,0),("pc",m,1),("grad",m,2)]
        for u in (0,1):
            for s in SIGNS:
                add(("yr", m, u, s, 2), name("y", s), 0.5, pcs)
                add(("yr", m, u, s, 1), name("y", s), 1.0, [("yr", m, u, s, 2)])
        for u in (0,1):
            fin = [("yr", m, u, s, 1) for s in SIGNS]
            for s in SIGNS:
                add(("yg", m, u, s, 1), name("y", s), 1.0, fin)
                add(("yg", m, u, s, 2), name("y", s), 0.5, [("yg", m, u, s, 1)])
            add(("cg", m, u, 0), "c", 0.2, fin)
            add(("cg", m, u, -1), "c", 0.2, [("yg", m, u, 1, 1)])
            add(("cg", m, u, 1), "c", 0.2, [("yg", m, u, -1, 1)])
            add(("cg", m, u, 2), "c", 0.2, [("yg", m, u, 1, 2), ("yg", m, u, -1, 2)])
    return items
def build_chunks(o, items):
    def all_of(kinds, p): return [k for k in items if k[0] in kinds and k[1] == p]
    ag = ("ax", "az", "bz", "bx")
    chunks = [(("load",), 0.3, [("count", "ag", 0, 30)])]
    chunks += [(("pre", i), 0.56, all_of(ag, 0) + [("load",)]) for i in range(4)]
    pre = [("pre", i) for i in range(4)]
    np=o["np"]; chunks += [(("out", dz, c), 10.0/8/np, pre) for dz in o["dzs"] for c in range(np)]
    agr = [("agrad", i) for i in range(4)]
    tail=[(("back",dz,c),10.6/8/np,agr) for dz in o["dzs"] for c in range(np)]
    ft=[(("fterm",i),.63,agr) for i in range(4)]
    st=[(("sterm",i),.5,all_of(ag,1)+pre) for i in range(4)]
    tail[o["pf"]:o["pf"]]=ft
    ps=o["ps"]
    if ps>=0: tail[ps:ps]=st
    ag_=[(("agrad",i),.55,all_of(ag,1)+pre) for i in range(4)]
    chunks += (st if ps<0 else [])+ag_+tail
    return chunks
def build_marks(o, items):
    final = [[("rx", q, s, 1) for s in SIGNS]+ [("rz", q, 0, s, 1) for s in SIGNS]+ [("sz", q, s, 1) for s in SIGNS]+ [("sx", q, 0, s, 1) for s in SIGNS] for q in (0, 1)]
    marks = [
        (("gate", "ag", 0), []),
        (("gate", "ag", 1), [("count", "ag", 0, o["g1"])]),
        (("gate", "rs", 0), [("count", "ag", 1, o["g2"])]),
        (("gate", "rs", 1), [("count", "rs", 0, o["g3"])]),
        (("gate2", "rs", 0), [("count", "rs", 0, o.get("h",0))]),
        (("gate2", "rs", 1), [("count", "rs", 1, o.get("h",0))]),
        (("store", 0), final[0]),(("store", 1), final[1]),
    ]
    for kd in ("out","back"):
        marks += [((kd,dz),[(kd,dz,c) for c in range(o["np"])]) for dz in DZ]
    for m,n in ((0,"sterm"),(1,"fterm")):
        marks += [(("grad", m, 0), [(n,0)]),(("grad", m, 1), [(n,1)]),(("grad", m, 2), [(n,i) for i in range(4)])]
        for u in (0,1): marks.append((("own",m,u),[("yr",m,u,s,1) for s in SIGNS]))
    return marks
def ranks(o, items):
    after={}
    for k,(_,_,deps) in items.items():
        for d in deps: after.setdefault(d,[]).append(k)
    left={}
    def way(k):
        if k not in left: left[k]=items[k][1]*o["UNIT"]+o["LAT"]+max([way(n) for n in after.get(k,[])]+[0.0])
        return left[k]
    def phase(k):
        g=GROUP.get(k[0],"ar")
        return k[1] if g=="ag" else 2+k[1] if g=="rs" else k[1]
    rnd=random.Random(o["seed"])
    return {k:(phase(k)*o["PH"]-way(k)+o["amp"]*rnd.random(),i) for i,k in enumerate(items)}
def build_order(o):
    items = build_items(o); chunks = build_chunks(o, items); marks = build_marks(o, items)
    UNIT,LAT=o["UNIT"],o["LAT"]
    got, counts, free = set(), {}, {}
    waiting = list(items); heap, order = [], []; now, seq = 0.0, 0
    pend={}; members={}; ready=[]; rank=ranks(o, items)
    for k in items: members[pair_of(k)]=members.get(pair_of(k),0)+1
    def met(need):
        if need[0] == "count": return counts.get((need[1], need[2]), 0) >= need[3]
        return need in got
    def settle():
        nonlocal now, seq
        moved = True
        while moved:
            moved = False
            for mark in list(marks):
                if all(met(n) for n in mark[1]):
                    marks.remove(mark); order.append(("mark", mark[0])); got.add(mark[0]); moved = True
            for key in list(waiting):
                if all(d in got for d in items[key][2]):
                    waiting.remove(key); ready.append(key)
            ready.sort(key=lambda k: rank[k])
            for key in list(ready):
                link, size, _ = items[key]
                if free.get(link, 0.0) - now < o["TH"]:
                    ready.remove(key); order.append(("send", key)); now += 0.03
                    start = max(now, free.get(link, 0.0))
                    free[link] = start + size * UNIT * o.get(link[0], 1.0); seq += 1
                    pair=pair_of(key); pend.setdefault(pair,[]).append(free[link]+LAT)
                    if len(pend[pair])==members[pair]: heapq.heappush(heap, (max(pend[pair]), seq, pair))
                    moved = True
    settle()
    held=[]
    while heap or chunks or held:
        key=None
        for h in held:
            if all(n in got for n in recv_need(h)): key=h; held.remove(h); break
        if key is None and heap and heap[0][0] <= now:
            key = heapq.heappop(heap)[2]
            if not all(n in got for n in recv_need(key)): held.append(key); continue
        if key is not None:
            order.append(("recv", key)); got.update(k for k in items if pair_of(k)==key)
            group = GROUP.get(key[0], "ar"); counts[(group, key[1])] = counts.get((group, key[1]), 0) + members[key]
            now += COST.get(group, 0.2); settle(); continue
        if chunks and all(met(n) for n in chunks[0][2]):
            key, time, _ = chunks.pop(0); order.append(("comp", key)); got.add(key); now += time
            settle(); continue
        if not heap: return None
        now = max(now, heap[0][0])
    if waiting or marks or ready: return None
    return list(items), order, now


KEYS, ORDER, SPAN = build_order(OPT)
PAIRS = list(dict.fromkeys(pair_of(k) for k in KEYS))


def semaphore_index():
    index, n = {}, {}
    for k in PAIRS:
        group = GROUP.get(k[0], "ar")
        slot = (group, k[1] if group != "ar" else 0)
        index[k] = n.get(slot, 0) + (76 if group == "ar" else 38 * k[1])
        n[slot] = n.get(slot, 0) + 1
    return index, max(index.values()) + 1


INDEX, NSEM = semaphore_index()


def slot_index():
    a, b, y = {}, {}, {}
    na = nb = ny = 0
    for k in PAIRS:
        split = k[-1] == (4 if k[0][-1] == "z" else 2)
        n = 1 if split else 2
        if k[0] in ("rz", "rx") and k[1] == 0:
            a[(k[0],) + k[2:]] = na
            na += n
        if k[0] in ("sx", "sz") and k[1] == 0:
            b[(k[0],) + k[2:]] = nb
            nb += n
        if k[0] == "yr" and k[1:3] == (0, 0):
            y[k[-1]] = ny
            ny += n
    return a, b, y, na, nb, ny


SLOT_A, SLOT_B, SLOT_Y, NA, NB, NYS = slot_index()
SENT = {"ag": (0, 1), "rs": (0, 1), "ar": (0, 1)}
SEND = {"ag": 0, "rs": 2, "pc": 4, "yr": 4, "yg": 6, "cg": 6}


def gelu_pair(value):
    inner = gelu_scale * (value + gelu_cube * value * value * value)
    tangent = jnp.tanh(inner)
    result = 0.5 * value * (1.0 + tangent)
    slope = 0.5 * (1.0 + tangent) + 0.5 * value * (1.0 - tangent * tangent) * gelu_scale * (
        1.0 + 3.0 * gelu_cube * value * value
    )
    return result, slope


def kernel(
    tokens, grads, pattern, first, second,
    out_ref, back_ref, fgrad_ref, sgrad_ref,
    xb, gb, part0, part1, slot_a, slot_b, w1, w2, act, pgrad, slope_ref,
    sgr, fgr, pair, yslot, patv, pats, invv, invs,
    send_sem, recv_sem, local_sem,
):
    t = lax.axis_index("tensor")
    d = lax.axis_index("dp")
    x, z = lax.div(t, NZ), lax.rem(t, NZ)
    y, core = lax.div(d, 2), lax.rem(d, 2)

    def at(dx, dz):
        return lax.rem(x + (dx + NX), NX) * NZ + lax.rem(z + (dz + NZ), NZ)

    def dev_x(s):
        return {"tensor": at(s, 0)}

    def dev_z(s):
        return {"tensor": at(0, s)}

    def dev_y(s):
        return {"dp": lax.rem(y + (s + NY), NY) * 2 + core}

    partner = {"dp": y * 2 + (1 - core)}
    base = core * 4

    def yrow(dy, b=None):
        return (base if b is None else b) + lax.rem(y + (dy + NY), NY)

    barrier = pltpu.get_barrier_semaphore()
    for dev in (dev_x(1), dev_x(-1), dev_z(1), dev_z(-1), dev_y(1), dev_y(-1), partner):
        pl.semaphore_signal(barrier, inc=1, device_id=dev, device_id_type=MESH)

    local = []
    for n, (src, buf) in enumerate(((tokens, xb), (grads, gb))):
        for h in (0, 1):
            c = pltpu.make_async_copy(
                src.at[:, pl.ds(h * BLK, BLK)], buf.at[t, h], local_sem.at[2 * n + h]
            )
            c.start()
            local.append(c)
    load_w1 = pltpu.make_async_copy(first, w1.at[:, pl.ds(0, K)], local_sem.at[4])
    load_w2 = pltpu.make_async_copy(second, w2.at[:, pl.ds(0, K)], local_sem.at[5])
    load_pat = [
        pltpu.make_async_copy(pattern, patv, local_sem.at[7]),
        pltpu.make_async_copy(pattern, pats, local_sem.at[8]),
    ]
    for c in load_pat:
        c.start()
    load_w1.start()
    load_w2.start()

    load_inv = pltpu.make_async_copy(invv, invs, local_sem.at[6])
    for c in local[:2]:
        c.wait()

    pl.semaphore_wait(barrier, 7)

    gathered = (xb, gb)
    parts = (part0, part1)
    grad_of = (sgr, fgr)
    grad_out = (sgrad_ref, fgrad_ref)

    def rows_of(key):
        n = SPLIT[key[1] + (0 if GROUP[key[0]] == "ag" else 2)]
        return (pl.ds(0, n), n) if key[0][0] in "ar" else (pl.ds(n, ROWS - n), ROWS - n)

    def half(s):
        return 0 if s > 0 else 1

    def reduce_slot(key):
        rows, n = rows_of(key)
        kind, q, s, k = key[0], key[1], key[-2], key[-1]
        sub = (kind,) + key[2:-2] + (k,)
        split = k == (4 if kind[1] == "z" else 2)
        lane = 0 if split or s > 0 else 1
        if kind[0] == "r":
            return rows, slot_a.at[q, SLOT_A[sub] + lane, :, pl.ds(0, n), :], split
        return rows, slot_b.at[q, SLOT_B[sub] + lane, :, pl.ds(0, n), :], split

    def reduce_shard(key, k):
        kind, s = key[0], key[-2]
        if kind == "rz":
            return at(key[2], s * k)
        if kind == "sz":
            return at(0, s * k)
        if kind == "rx":
            return at(s * k, 0)
        return at(s * k, key[2])

    def copy_of(key):
        kind, p = key[0], key[1]
        group = GROUP.get(kind, kind)
        ss, rs = send_sem.at[SEND[group] + p], recv_sem.at[INDEX[pair_of(key)]]

        def remote(src, dst, dev):
            return pltpu.make_async_remote_copy(
                src_ref=src, dst_ref=dst, send_sem=ss, recv_sem=rs, device_id=dev, device_id_type=MESH
            )

        if group == "ag":
            s, k = key[-2], key[-1]
            rows = rows_of(key)[0]
            if kind == "ax":
                own, dev, split = at(-s * (k - 1), 0), dev_x(s), k == 2
            elif kind == "az":
                own, dev, split = at(key[2], -s * (k - 1)), dev_z(s), k == 4
            elif kind == "bz":
                own, dev, split = at(0, -s * (k - 1)), dev_z(s), k == 4
            else:
                own, dev, split = at(-s * (k - 1), key[2]), dev_x(s), k == 2
            view = gathered[p].at[own, pl.ds(half(s), 1) if split else pl.ds(0, 2), rows, :]
            return remote(view, view, dev)
        if group == "rs":
            s, k = key[-2], key[-1]
            rows, slot, split = reduce_slot(key)
            hs = pl.ds(half(s), 1) if split else pl.ds(0, 2)
            dev = dev_z(s) if kind[1] == "z" else dev_x(s)
            return remote(parts[p].at[reduce_shard(key, k), hs, rows, :], slot.at[hs], dev)
        g, out = grad_of[p], grad_out[p]
        if kind == "pc":
            v = key[2] * 2
            return remote(g.at[pl.ds((1 - core) * 4 + v, 2)], pair.at[p, pl.ds(v, 2)], partner)
        u, s, k = key[2] * 4, key[-2], key[-1]
        if kind == "cg":
            js, dy = pl.ds(u, 4), key[3]
            src = g.at[yrow(0), js] if dy == 0 else out.at[yrow(dy), js]
            return remote(src, out.at[yrow(dy), js], partner)
        js = pl.ds(u + half(s) * 2, 2) if k == 2 else pl.ds(u, 4)
        if kind == "yr":
            slot = SLOT_Y[k] + (0 if k == 2 or s > 0 else 1)
            return remote(g.at[yrow(s * k), js], yslot.at[p, slot, js], dev_y(s))
        src = g.at[yrow(0), js] if k == 1 else out.at[yrow(-s), js]
        return remote(src, out.at[yrow(-s * (k - 1)), js], dev_y(s))

    def wait_for(view, sem, sent=False):
        c = pltpu.make_async_remote_copy(
            src_ref=view, dst_ref=view, send_sem=sem, recv_sem=sem, device_id=partner, device_id_type=MESH
        )
        if sent:
            c.wait_send()
        else:
            c.wait_recv()

    def received(key):
        kind, p = key[0], key[1]
        sem = recv_sem.at[INDEX[key]]
        group = GROUP.get(kind, kind)
        if group == "ag":
            rows = rows_of(key)[0]
            split = key[-1] == (4 if kind[1] == "z" else 2)
            wait_for(gathered[p].at[pl.ds(0, 1 if split else 2), :, rows, :], sem)
        elif group == "rs":
            split = key[-1] == (4 if kind[1] == "z" else 2)
            signed = [key[:-1] + (s, key[-1]) for s in SIGNS]
            rows = rows_of(key)[0]
            wait_for(parts[p].at[pl.ds(0, 1 if split else 2), :, rows, :], sem)
            places = [reduce_shard(k, key[-1] - 1) for k in signed]
            slots = [reduce_slot(k)[1] for k in signed]
            if key[-1] == 1:
                for h in (0, 1):
                    total = parts[p][places[0], h, rows, :].astype(F32)
                    total = total + slots[0][h].astype(F32) + slots[1][h].astype(F32)
                    parts[p][places[0], h, rows, :] = total.astype(BF)
                return
            for s, mine, slot in zip(SIGNS, places, slots):
                for h in (half(s),) if split else (0, 1):
                    parts[p][mine, h, rows, :] = parts[p][mine, h, rows, :] + slot[h]
        elif kind == "pc":
            v = key[2] * 2
            g = grad_of[p]
            wait_for(pair.at[p, pl.ds(v, 2)], sem)

            @pl.loop(v, v + 2)
            def _(r):
                @pl.loop(0, K)
                def _(j):
                    total = g[base + r, j] + pair[p, r, j]
                    g[base + r, j] = total
        elif kind == "yr":
            u, k = key[2] * 4, key[-1]
            g = grad_of[p]
            if k == 2:
                wait_for(yslot.at[p, SLOT_Y[2], pl.ds(u, 4)], sem)
                for s in SIGNS:
                    row = yrow(s)
                    lo = u + half(s) * 2

                    @pl.loop(lo, lo + 2)
                    def _(j):
                        total = g[row, j] + yslot[p, SLOT_Y[2], j]
                        g[row, j] = total
            else:
                wait_for(yslot.at[p, pl.ds(SLOT_Y[1], 2), pl.ds(u, 4)], sem)
                row = yrow(0)

                @pl.loop(u, u + 4)
                def _(j):
                    total = g[row, j].astype(F32) + yslot[p, SLOT_Y[1], j].astype(F32)
                    total = total + yslot[p, SLOT_Y[1] + 1, j].astype(F32)
                    g[row, j] = total.astype(BF)
        elif kind == "yg":
            wait_for(grad_out[p].at[pl.ds(0, 2 if key[-1] == 1 else 1), pl.ds(key[2] * 4, 4)], sem)
        else:
            wait_for(grad_out[p].at[pl.ds(0, 4)], sem)

    def picked(buf, r):
        return jnp.concatenate([buf[lax.div(pats[r, j], 2), lax.rem(pats[r, j], 2)] for j in range(K)], axis=1)

    def whole(ref):
        return jnp.concatenate([ref[r] for r in range(HR)], axis=1)

    nt = (((1,), (1,)), ((), ()))

    def compute(key):
        kind = key[0]
        if kind == "load":
            for c in load_pat:
                c.wait()
            cols = lax.broadcasted_iota(jnp.int32, (HR, BLK), 1)
            inv = jnp.full((HR, BLK), K, jnp.int32)
            for j in range(K):
                inv = jnp.where(patv[:, j : j + 1] == cols, j, inv)
            invv[...] = inv
            load_inv.start()
            load_w1.wait()
            load_w2.wait()
            load_inv.wait()
            for w in (w1, w2):
                for r in range(HR):
                    w[r, K] = jnp.zeros((BLK, BLK), BF)
            return
        i = key[1]
        if kind in ("out", "back"):

            per = NX // OPT["np"]

            @pl.loop(key[2] * per, key[2] * per + per)
            def _(dx):
                dest = lax.rem(x + dx, NX) * NZ + lax.rem(z + (i + NZ), NZ)
                if kind == "out":
                    rhs = jnp.concatenate(
                        [
                            jnp.concatenate([w2[r, invs[r, 2 * dest + h]] for r in range(HR)], axis=0)
                            for h in (0, 1)
                        ],
                        axis=1,
                    )
                    res = jnp.dot(whole(act), rhs, preferred_element_type=F32)
                else:
                    rhs = jnp.concatenate(
                        [
                            jnp.concatenate([w1[r, invs[r, 2 * dest + h]] for r in range(HR)], axis=1)
                            for h in (0, 1)
                        ],
                        axis=0,
                    )
                    res = lax.dot_general(whole(pgrad), rhs, nt, preferred_element_type=F32)
                buf = part0 if kind == "out" else part1
                for h in (0, 1):
                    buf[dest, h] = res[:, h * BLK : (h + 1) * BLK].astype(BF)

            return

        @pl.loop(i * 2, i * 2 + 2)
        def _(n):
            r = lax.rem((1 - core) * 4 + n, HR)
            if kind == "pre":
                weights = jnp.concatenate([w1[r, j] for j in range(K)], axis=0)
                pre = jnp.dot(picked(xb, r), weights, preferred_element_type=F32)
                value, slope = gelu_pair(pre)
                act[r] = value.astype(BF)
                slope_ref[r] = slope
            elif kind == "sterm":
                res = jnp.dot(act[r].T, picked(gb, r), preferred_element_type=F32)
                for j in range(K):
                    sgr[r, j] = res[:, j * BLK : (j + 1) * BLK].astype(BF)
            elif kind == "agrad":
                weights = jnp.concatenate([w2[r, j] for j in range(K)], axis=1)
                res = lax.dot_general(picked(gb, r), weights, nt, preferred_element_type=F32)
                pgrad[r] = (res * slope_ref[r]).astype(BF)
            elif kind == "fterm":
                res = jnp.dot(pgrad[r].T, picked(xb, r), preferred_element_type=F32)
                for j in range(K):
                    fgr[r, j] = res[:, j * BLK : (j + 1) * BLK].astype(BF).T

    stores = []

    def store(src, dst):
        c = pltpu.make_async_copy(src, dst, local_sem.at[9 + len(stores)])
        c.start()
        stores.append(c)

    def marked(key):
        if key == ("gate", "ag", 1):
            for c in local[2:]:
                c.wait()
        if key[0] == "store":
            q = key[1]
            dst = (out_ref, back_ref)[q]
            for h in (0, 1):
                dst[:, h * BLK : (h + 1) * BLK] = parts[q][t, h]
        elif key[0] == "own":
            m, js = key[1], pl.ds(key[2] * 4, 4)
            store(grad_of[m].at[yrow(0), js], grad_out[m].at[yrow(0), js])

    for action, key in ORDER:
        if action == "send":
            copy_of(key).start()
        elif action == "recv":
            received(key)
        elif action == "comp":
            compute(key)
        else:
            marked(key)
    for p in (0, 1):
        if p in SENT["ag"]:
            wait_for(gathered[p].at[pl.ds(0, 31)], send_sem.at[SEND["ag"] + p], True)
        if p in SENT["rs"]:
            wait_for(parts[p].at[pl.ds(0, 31)], send_sem.at[SEND["rs"] + p], True)
        if p in SENT["ar"]:
            wait_for(grad_of[p].at[pl.ds(0, 7)], send_sem.at[SEND["yr"] + p], True)
            wait_for(grad_of[p].at[pl.ds(0, 7)], send_sem.at[SEND["yg"] + p], True)
    for c in stores:
        c.wait()


def finish(*refs):
    srcs, dsts, sem = refs[:4], refs[4:8], refs[8]
    copies = [pltpu.make_async_copy(src, dst, sem.at[i]) for i, (src, dst) in enumerate(zip(srcs, dsts))]
    for c in copies:
        c.start()
    for c in copies:
        c.wait()


def shards(tokens, pattern, first_blocks, second_blocks, out_grad):
    any_space = pl.BlockSpec(memory_space=pltpu.HBM)
    n = NSEM
    shapes = (
            jax.ShapeDtypeStruct(tokens.shape, BF),
            jax.ShapeDtypeStruct(tokens.shape, BF),
            jax.ShapeDtypeStruct(first_blocks.shape, BF),
            jax.ShapeDtypeStruct(second_blocks.shape, BF),
        )
    results = pl.pallas_call(
        kernel,
        out_shape=tuple(pltpu.VMEM(r.shape, BF) for r in shapes),
        in_specs=[
            any_space,
            any_space,
            any_space,
            any_space,
            any_space,
        ],
        out_specs=(pl.BlockSpec(memory_space=pltpu.VMEM),) * 4,
        scratch_shapes=[
            pltpu.VMEM((32, 2, ROWS, BLK), BF),
            pltpu.VMEM((32, 2, ROWS, BLK), BF),
            pltpu.VMEM((32, 2, ROWS, BLK), BF),
            pltpu.VMEM((32, 2, ROWS, BLK), BF),
            pltpu.VMEM((2, NA, 2, RA, BLK), BF),
            pltpu.VMEM((2, NB, 2, RB, BLK), BF),
            pltpu.VMEM((HR, K + 1, BLK, BLK), BF),
            pltpu.VMEM((HR, K + 1, BLK, BLK), BF),
            pltpu.VMEM((HR, ROWS, BLK), BF),
            pltpu.VMEM((HR, ROWS, BLK), BF),
            pltpu.VMEM((HR, ROWS, BLK), F32),
            pltpu.VMEM((HR, K, BLK, BLK), BF),
            pltpu.VMEM((HR, K, BLK, BLK), BF),
            pltpu.VMEM((2, 4, K, BLK, BLK), BF),
            pltpu.VMEM((2, NYS, K, BLK, BLK), BF),
            pltpu.VMEM((HR, K), jnp.int32),
            pltpu.SMEM((HR, K), jnp.int32),
            pltpu.VMEM((HR, BLK), jnp.int32),
            pltpu.SMEM((HR, BLK), jnp.int32),
            pltpu.SemaphoreType.DMA((8,)),
            pltpu.SemaphoreType.DMA((n,)),
            pltpu.SemaphoreType.DMA((13,)),
        ],
        compiler_params=pltpu.CompilerParams(
            collective_id=0, has_side_effects=True, vmem_limit_bytes=62500000
        ),
    )(tokens, out_grad, pattern, first_blocks, second_blocks)
    return pl.pallas_call(
        finish,
        out_shape=shapes,
        in_specs=[pl.BlockSpec(memory_space=pltpu.VMEM)] * 4,
        out_specs=(any_space,) * 4,
        scratch_shapes=[pltpu.SemaphoreType.DMA((4,))],
        compiler_params=pltpu.CompilerParams(vmem_limit_bytes=4 * 1024 * 1024),
    )(*[pltpu.with_memory_space_constraint(r, pltpu.VMEM) for r in results])


def solution(mesh):
    placed = (
        P("dp", "tensor"),
        P("tensor", None),
        P("tensor", None, None, None),
        P("tensor", None, None, None),
        P("dp", "tensor"),
    )
    return jax.shard_map(
        shards,
        mesh=mesh,
        in_specs=placed,
        out_specs=(
            P("dp", "tensor"),
            P("dp", "tensor"),
            P("tensor", None, None, None),
            P("tensor", None, None, None),
        ),
        check_vma=False,
    )
```

```python
import heapq
import random

import jax
import jax.numpy as jnp
from jax import lax
from jax.experimental import pallas as pl
from jax.experimental.pallas import tpu as pltpu
from jax.sharding import PartitionSpec as P

MESH = pl.DeviceIdType.MESH
BF = jnp.bfloat16
F32 = jnp.float32

gelu_scale = 0.7978845608028654
gelu_cube = 0.044715

NX, NZ, NY = 4, 8, 4
ROWS, BLK, HR, K = 256, 128, 8, 8
SIGNS = (1, -1)


OPT = dict(
    ra=(80, 112, 112, 96),
    UNIT=2.75,
    LAT=2.5,
    TH=1.5,
    PH=30,
    np=1,
    seed=4972,
    amp=4,
    y=0.93,
    g1=4,
    g2=52,
    g3=32,
    dzs=(4, 3, -3, 2, -2, 1, -1, 0),
    dxs=(2, 1, -1, 0),
    pf=0,
    ps=-1,
    cl=0.8,
    h=16,
    late_dx=(),
    late_dz=(0,),
)
SPLIT = OPT["ra"]
RA, RB = max(SPLIT), ROWS - min(SPLIT)
GROUP = {k: "ag" for k in ("ax", "az", "bz", "bx")} | {k: "rs" for k in ("rz", "rx", "sx", "sz")}
COST = {"ag": 0.03, "rs": 0.16}


def name(axis, s):
    return axis + ("+" if s > 0 else "-")


DZ=(4,3,-3,2,-2,1,-1,0)
def nz(dz): return 4 if dz==-4 else dz
def pair_of(key):
    if key[0]=="pc": return key
    if key[0]=="cg": return key[:2]
    return key[:-2]+key[-1:]
def recv_need(key):
    kind="out" if key[1]==0 else "back"
    if key[0] in ("rz","sz"): return [(kind, nz(c*(key[-1]-1))) for c in SIGNS]
    if key[0]=="rx": return [(kind,0)]
    if key[0]=="sx": return [(kind,key[2])]
    if key[0]=="pc": return [("grad",key[1],2)]
    return []
def build_items(o):
    items={}
    def add(key, link, size, deps): items[key]=(link,size,tuple(deps))
    for p in (0, 1):
        gate = [("gate", "ag", p)]
        fa = o["ra"][p] / ROWS
        fb = 1 - fa
        for s in SIGNS:
            add(("bz", p, s, 1), name("z", s), fb, gate)
            add(("ax", p, s, 1), name("x", s), fa, gate)
        for s in SIGNS:
            add(("az", p, 0, s, 1), name("z", s), fa, gate)
            add(("bx", p, 0, s, 1), name("x", s), fb, gate)
        for s in SIGNS:
            add(("ax", p, s, 2), name("x", s), fa / 2, [("ax", p, s, 1)])
            for k in (2, 3, 4):
                add(("bz", p, s, k), name("z", s), fb if k < 4 else fb / 2, [("bz", p, s, k - 1)])
        for dx, ready in ((0, gate),(-1, [("ax", p, 1, 1)]),(1, [("ax", p, -1, 1)]),(2, [("ax", p, 1, 2), ("ax", p, -1, 2)])):
            for s in SIGNS:
                for k in (1, 2, 3, 4):
                    add(("az", p, dx, s, k), name("z", s), fa if k < 4 else fa / 2, ready if k == 1 else [("az", p, dx, s, k - 1)])
        for dz in (0, -1, 1, -2, 2, -3, 3, 4):
            if dz == 0: ready = gate
            elif dz == 4: ready = [("bz", p, 1, 4), ("bz", p, -1, 4)]
            else: ready = [("bz", p, 1 if dz < 0 else -1, abs(dz))]
            for s in SIGNS:
                add(("bx", p, dz, s, 1), name("x", s), fb, ready)
                add(("bx", p, dz, s, 2), name("x", s), fb / 2, [("bx", p, dz, s, 1)])
    for q in (0, 1):
        kd="out" if q==0 else "back"
        fa = o["ra"][2 + q] / ROWS
        fb = 1 - fa
        def gate(c): return [("gate","rs",q)] + ([("gate2","rs",q)] if c else [])
        def done_a(dx): return [("rz", q, dx, s, 1) for s in SIGNS]
        def done_b(dz): return [("sx", q, dz, s, 1) for s in SIGNS]
        for dx in o["dxs"]:
            for s in SIGNS:
                for k in (4, 3, 2, 1):
                    add(("rz", q, dx, s, k), name("z", s), fa if k < 4 else fa / 2, (gate(dx in o.get("late_dx",())) if k == 4 else [("rz", q, dx, s, k + 1)])+[(kd,nz(s*k))])
        for dz in o["dzs"]:
            for s in SIGNS:
                add(("sx", q, dz, s, 2), name("x", s), fb / 2, gate(dz in o.get("late_dz",()))+[(kd,dz)])
                add(("sx", q, dz, s, 1), name("x", s), fb, [("sx", q, dz, s, 2)])
        for s in SIGNS:
            add(("rx", q, s, 2), name("x", s), fa / 2, done_a(2))
            add(("rx", q, s, 1), name("x", s), fa, [("rx", q, s, 2)] + done_a(s))
            add(("sz", q, s, 4), name("z", s), fb / 2, done_b(4))
            for k in (3, 2, 1):
                add(("sz", q, s, k), name("z", s), fb, [("sz", q, s, k + 1)] + done_b(s * k))
    for m in (0, 1):
        for v in (0,1):
            add(("pc", m, v), "c", o["cl"]/2, [("grad", m, v)])
        pcs=[("pc",m,0),("pc",m,1),("grad",m,2)]
        for u in (0,1):
            for s in SIGNS:
                add(("yr", m, u, s, 2), name("y", s), 0.5, pcs)
                add(("yr", m, u, s, 1), name("y", s), 1.0, [("yr", m, u, s, 2)])
        for u in (0,1):
            fin = [("yr", m, u, s, 1) for s in SIGNS]
            for s in SIGNS:
                add(("yg", m, u, s, 1), name("y", s), 1.0, fin)
                add(("yg", m, u, s, 2), name("y", s), 0.5, [("yg", m, u, s, 1)])
            add(("cg", m, u, 0), "c", 0.2, fin)
            add(("cg", m, u, -1), "c", 0.2, [("yg", m, u, 1, 1)])
            add(("cg", m, u, 1), "c", 0.2, [("yg", m, u, -1, 1)])
            add(("cg", m, u, 2), "c", 0.2, [("yg", m, u, 1, 2), ("yg", m, u, -1, 2)])
    return items
def build_chunks(o, items):
    def all_of(kinds, p): return [k for k in items if k[0] in kinds and k[1] == p]
    ag = ("ax", "az", "bz", "bx")
    chunks = [(("load",), 0.3, [("count", "ag", 0, 30)])]
    chunks += [(("pre", i), 0.56, all_of(ag, 0) + [("load",)]) for i in range(4)]
    pre = [("pre", i) for i in range(4)]
    np=o["np"]; chunks += [(("out", dz, c), 10.0/8/np, pre) for dz in o["dzs"] for c in range(np)]
    agr = [("agrad", i) for i in range(4)]
    tail=[(("back",dz,c),10.6/8/np,agr) for dz in o["dzs"] for c in range(np)]
    ft=[(("fterm",i),.63,agr) for i in range(4)]
    st=[(("sterm",i),.5,all_of(ag,1)+pre) for i in range(4)]
    tail[o["pf"]:o["pf"]]=ft
    ps=o["ps"]
    if ps>=0: tail[ps:ps]=st
    ag_=[(("agrad",i),.55,all_of(ag,1)+pre) for i in range(4)]
    chunks += (st if ps<0 else [])+ag_+tail
    return chunks
def build_marks(o, items):
    final = [[("rx", q, s, 1) for s in SIGNS]+ [("rz", q, 0, s, 1) for s in SIGNS]+ [("sz", q, s, 1) for s in SIGNS]+ [("sx", q, 0, s, 1) for s in SIGNS] for q in (0, 1)]
    marks = [
        (("gate", "ag", 0), []),
        (("gate", "ag", 1), [("count", "ag", 0, o["g1"])]),
        (("gate", "rs", 0), [("count", "ag", 1, o["g2"])]),
        (("gate", "rs", 1), [("count", "rs", 0, o["g3"])]),
        (("gate2", "rs", 0), [("count", "rs", 0, o.get("h",0))]),
        (("gate2", "rs", 1), [("count", "rs", 1, o.get("h",0))]),
        (("store", 0), final[0]),(("store", 1), final[1]),
    ]
    for kd in ("out","back"):
        marks += [((kd,dz),[(kd,dz,c) for c in range(o["np"])]) for dz in DZ]
    for m,n in ((0,"sterm"),(1,"fterm")):
        marks += [(("grad", m, 0), [(n,0)]),(("grad", m, 1), [(n,1)]),(("grad", m, 2), [(n,i) for i in range(4)])]
        for u in (0,1): marks.append((("own",m,u),[("yr",m,u,s,1) for s in SIGNS]))
    return marks
def ranks(o, items):
    after={}
    for k,(_,_,deps) in items.items():
        for d in deps: after.setdefault(d,[]).append(k)
    left={}
    def way(k):
        if k not in left: left[k]=items[k][1]*o["UNIT"]+o["LAT"]+max([way(n) for n in after.get(k,[])]+[0.0])
        return left[k]
    def phase(k):
        g=GROUP.get(k[0],"ar")
        return k[1] if g=="ag" else 2+k[1] if g=="rs" else k[1]
    rnd=random.Random(o["seed"])
    return {k:(phase(k)*o["PH"]-way(k)+o["amp"]*rnd.random(),i) for i,k in enumerate(items)}
def build_order(o):
    items = build_items(o); chunks = build_chunks(o, items); marks = build_marks(o, items)
    UNIT,LAT=o["UNIT"],o["LAT"]
    got, counts, free = set(), {}, {}
    waiting = list(items); heap, order = [], []; now, seq = 0.0, 0
    pend={}; members={}; ready=[]; rank=ranks(o, items)
    for k in items: members[pair_of(k)]=members.get(pair_of(k),0)+1
    def met(need):
        if need[0] == "count": return counts.get((need[1], need[2]), 0) >= need[3]
        return need in got
    def settle():
        nonlocal now, seq
        moved = True
        while moved:
            moved = False
            for mark in list(marks):
                if all(met(n) for n in mark[1]):
                    marks.remove(mark); order.append(("mark", mark[0])); got.add(mark[0]); moved = True
            for key in list(waiting):
                if all(d in got for d in items[key][2]):
                    waiting.remove(key); ready.append(key)
            ready.sort(key=lambda k: rank[k])
            for key in list(ready):
                link, size, _ = items[key]
                if free.get(link, 0.0) - now < o["TH"]:
                    ready.remove(key); order.append(("send", key)); now += 0.03
                    start = max(now, free.get(link, 0.0))
                    free[link] = start + size * UNIT * o.get(link[0], 1.0); seq += 1
                    pair=pair_of(key); pend.setdefault(pair,[]).append(free[link]+LAT)
                    if len(pend[pair])==members[pair]: heapq.heappush(heap, (max(pend[pair]), seq, pair))
                    moved = True
    settle()
    held=[]
    while heap or chunks or held:
        key=None
        for h in held:
            if all(n in got for n in recv_need(h)): key=h; held.remove(h); break
        if key is None and heap and heap[0][0] <= now:
            key = heapq.heappop(heap)[2]
            if not all(n in got for n in recv_need(key)): held.append(key); continue
        if key is not None:
            order.append(("recv", key)); got.update(k for k in items if pair_of(k)==key)
            group = GROUP.get(key[0], "ar"); counts[(group, key[1])] = counts.get((group, key[1]), 0) + members[key]
            now += COST.get(group, 0.2); settle(); continue
        if chunks and all(met(n) for n in chunks[0][2]):
            key, time, _ = chunks.pop(0); order.append(("comp", key)); got.add(key); now += time
            settle(); continue
        if not heap: return None
        now = max(now, heap[0][0])
    if waiting or marks or ready: return None
    return list(items), order, now


KEYS, ORDER, SPAN = build_order(OPT)
PAIRS = list(dict.fromkeys(pair_of(k) for k in KEYS))


def semaphore_index():
    index, n = {}, {}
    for k in PAIRS:
        group = GROUP.get(k[0], "ar")
        slot = (group, k[1] if group != "ar" else 0)
        index[k] = n.get(slot, 0) + (76 if group == "ar" else 38 * k[1])
        n[slot] = n.get(slot, 0) + 1
    return index, max(index.values()) + 1


INDEX, NSEM = semaphore_index()


def slot_index():
    a, b, y = {}, {}, {}
    na = nb = ny = 0
    for k in PAIRS:
        split = k[-1] == (4 if k[0][-1] == "z" else 2)
        n = 1 if split else 2
        if k[0] in ("rz", "rx") and k[1] == 0:
            a[(k[0],) + k[2:]] = na
            na += n
        if k[0] in ("sx", "sz") and k[1] == 0:
            b[(k[0],) + k[2:]] = nb
            nb += n
        if k[0] == "yr" and k[1:3] == (0, 0):
            y[k[-1]] = ny
            ny += n
    return a, b, y, na, nb, ny


SLOT_A, SLOT_B, SLOT_Y, NA, NB, NYS = slot_index()
SENT = {"ag": (0, 1), "rs": (0, 1), "ar": (0, 1)}
SEND = {"ag": 0, "rs": 2, "pc": 4, "yr": 4, "yg": 6, "cg": 6}


def gelu_pair(value):
    inner = gelu_scale * (value + gelu_cube * value * value * value)
    tangent = jnp.tanh(inner)
    result = 0.5 * value * (1.0 + tangent)
    slope = 0.5 * (1.0 + tangent) + 0.5 * value * (1.0 - tangent * tangent) * gelu_scale * (
        1.0 + 3.0 * gelu_cube * value * value
    )
    return result, slope


def kernel(
    tokens, grads, pattern, first, second,
    out_ref, back_ref, fgrad_ref, sgrad_ref,
    xb, gb, part0, part1, slot_a, slot_b, w1, w2, act, pgrad, slope_ref,
    sgr, fgr, pair, yslot, patv, pats, invv, invs,
    send_sem, recv_sem, local_sem,
):
    t = lax.axis_index("tensor")
    d = lax.axis_index("dp")
    x, z = lax.div(t, NZ), lax.rem(t, NZ)
    y, core = lax.div(d, 2), lax.rem(d, 2)

    def at(dx, dz):
        return lax.rem(x + (dx + NX), NX) * NZ + lax.rem(z + (dz + NZ), NZ)

    def dev_x(s):
        return {"tensor": at(s, 0)}

    def dev_z(s):
        return {"tensor": at(0, s)}

    def dev_y(s):
        return {"dp": lax.rem(y + (s + NY), NY) * 2 + core}

    partner = {"dp": y * 2 + (1 - core)}
    base = core * 4

    def yrow(dy, b=None):
        return (base if b is None else b) + lax.rem(y + (dy + NY), NY)

    barrier = pltpu.get_barrier_semaphore()
    for dev in (dev_x(1), dev_x(-1), dev_z(1), dev_z(-1), dev_y(1), dev_y(-1), partner):
        pl.semaphore_signal(barrier, inc=1, device_id=dev, device_id_type=MESH)

    local = []
    for n, (src, buf) in enumerate(((tokens, xb), (grads, gb))):
        for h in (0, 1):
            c = pltpu.make_async_copy(
                src.at[:, pl.ds(h * BLK, BLK)], buf.at[t, h], local_sem.at[2 * n + h]
            )
            c.start()
            local.append(c)
    load_w1 = pltpu.make_async_copy(first, w1.at[:, pl.ds(0, K)], local_sem.at[4])
    load_w2 = pltpu.make_async_copy(second, w2.at[:, pl.ds(0, K)], local_sem.at[5])
    load_pat = [
        pltpu.make_async_copy(pattern, patv, local_sem.at[7]),
        pltpu.make_async_copy(pattern, pats, local_sem.at[8]),
    ]
    for c in load_pat:
        c.start()
    load_w1.start()
    load_w2.start()

    load_inv = pltpu.make_async_copy(invv, invs, local_sem.at[6])
    for c in local[:2]:
        c.wait()

    pl.semaphore_wait(barrier, 7)

    gathered = (xb, gb)
    parts = (part0, part1)
    grad_of = (sgr, fgr)
    grad_out = (sgrad_ref, fgrad_ref)

    def rows_of(key):
        n = SPLIT[key[1] + (0 if GROUP[key[0]] == "ag" else 2)]
        return (pl.ds(0, n), n) if key[0][0] in "ar" else (pl.ds(n, ROWS - n), ROWS - n)

    def half(s):
        return 0 if s > 0 else 1

    def reduce_slot(key):
        rows, n = rows_of(key)
        kind, q, s, k = key[0], key[1], key[-2], key[-1]
        sub = (kind,) + key[2:-2] + (k,)
        split = k == (4 if kind[1] == "z" else 2)
        lane = 0 if split or s > 0 else 1
        if kind[0] == "r":
            return rows, slot_a.at[q, SLOT_A[sub] + lane, :, pl.ds(0, n), :], split
        return rows, slot_b.at[q, SLOT_B[sub] + lane, :, pl.ds(0, n), :], split

    def reduce_shard(key, k):
        kind, s = key[0], key[-2]
        if kind == "rz":
            return at(key[2], s * k)
        if kind == "sz":
            return at(0, s * k)
        if kind == "rx":
            return at(s * k, 0)
        return at(s * k, key[2])

    def copy_of(key):
        kind, p = key[0], key[1]
        group = GROUP.get(kind, kind)
        ss, rs = send_sem.at[SEND[group] + p], recv_sem.at[INDEX[pair_of(key)]]

        def remote(src, dst, dev):
            return pltpu.make_async_remote_copy(
                src_ref=src, dst_ref=dst, send_sem=ss, recv_sem=rs, device_id=dev, device_id_type=MESH
            )

        if group == "ag":
            s, k = key[-2], key[-1]
            rows = rows_of(key)[0]
            if kind == "ax":
                own, dev, split = at(-s * (k - 1), 0), dev_x(s), k == 2
            elif kind == "az":
                own, dev, split = at(key[2], -s * (k - 1)), dev_z(s), k == 4
            elif kind == "bz":
                own, dev, split = at(0, -s * (k - 1)), dev_z(s), k == 4
            else:
                own, dev, split = at(-s * (k - 1), key[2]), dev_x(s), k == 2
            view = gathered[p].at[own, pl.ds(half(s), 1) if split else pl.ds(0, 2), rows, :]
            return remote(view, view, dev)
        if group == "rs":
            s, k = key[-2], key[-1]
            rows, slot, split = reduce_slot(key)
            hs = pl.ds(half(s), 1) if split else pl.ds(0, 2)
            dev = dev_z(s) if kind[1] == "z" else dev_x(s)
            return remote(parts[p].at[reduce_shard(key, k), hs, rows, :], slot.at[hs], dev)
        g, out = grad_of[p], grad_out[p]
        if kind == "pc":
            v = key[2] * 2
            return remote(g.at[pl.ds((1 - core) * 4 + v, 2)], pair.at[p, pl.ds(v, 2)], partner)
        u, s, k = key[2] * 4, key[-2], key[-1]
        if kind == "cg":
            js, dy = pl.ds(u, 4), key[3]
            src = g.at[yrow(0), js] if dy == 0 else out.at[yrow(dy), js]
            return remote(src, out.at[yrow(dy), js], partner)
        js = pl.ds(u + half(s) * 2, 2) if k == 2 else pl.ds(u, 4)
        if kind == "yr":
            slot = SLOT_Y[k] + (0 if k == 2 or s > 0 else 1)
            return remote(g.at[yrow(s * k), js], yslot.at[p, slot, js], dev_y(s))
        src = g.at[yrow(0), js] if k == 1 else out.at[yrow(-s), js]
        return remote(src, out.at[yrow(-s * (k - 1)), js], dev_y(s))

    def wait_for(view, sem, sent=False):
        c = pltpu.make_async_remote_copy(
            src_ref=view, dst_ref=view, send_sem=sem, recv_sem=sem, device_id=partner, device_id_type=MESH
        )
        if sent:
            c.wait_send()
        else:
            c.wait_recv()

    def received(key):
        kind, p = key[0], key[1]
        sem = recv_sem.at[INDEX[key]]
        group = GROUP.get(kind, kind)
        if group == "ag":
            rows = rows_of(key)[0]
            split = key[-1] == (4 if kind[1] == "z" else 2)
            wait_for(gathered[p].at[pl.ds(0, 1 if split else 2), :, rows, :], sem)
        elif group == "rs":
            split = key[-1] == (4 if kind[1] == "z" else 2)
            signed = [key[:-1] + (s, key[-1]) for s in SIGNS]
            rows = rows_of(key)[0]
            wait_for(parts[p].at[pl.ds(0, 1 if split else 2), :, rows, :], sem)
            places = [reduce_shard(k, key[-1] - 1) for k in signed]
            slots = [reduce_slot(k)[1] for k in signed]
            if key[-1] == 1:
                for h in (0, 1):
                    total = parts[p][places[0], h, rows, :].astype(F32)
                    total = total + slots[0][h].astype(F32) + slots[1][h].astype(F32)
                    parts[p][places[0], h, rows, :] = total.astype(BF)
                return
            for s, mine, slot in zip(SIGNS, places, slots):
                for h in (half(s),) if split else (0, 1):
                    parts[p][mine, h, rows, :] = parts[p][mine, h, rows, :] + slot[h]
        elif kind == "pc":
            v = key[2] * 2
            g = grad_of[p]
            wait_for(pair.at[p, pl.ds(v, 2)], sem)

            @pl.loop(v, v + 2)
            def _(r):
                @pl.loop(0, K)
                def _(j):
                    total = g[base + r, j] + pair[p, r, j]
                    g[base + r, j] = total
        elif kind == "yr":
            u, k = key[2] * 4, key[-1]
            g = grad_of[p]
            if k == 2:
                wait_for(yslot.at[p, SLOT_Y[2], pl.ds(u, 4)], sem)
                for s in SIGNS:
                    row = yrow(s)
                    lo = u + half(s) * 2

                    @pl.loop(lo, lo + 2)
                    def _(j):
                        total = g[row, j] + yslot[p, SLOT_Y[2], j]
                        g[row, j] = total
            else:
                wait_for(yslot.at[p, pl.ds(SLOT_Y[1], 2), pl.ds(u, 4)], sem)
                row = yrow(0)

                @pl.loop(u, u + 4)
                def _(j):
                    total = g[row, j].astype(F32) + yslot[p, SLOT_Y[1], j].astype(F32)
                    total = total + yslot[p, SLOT_Y[1] + 1, j].astype(F32)
                    g[row, j] = total.astype(BF)
        elif kind == "yg":
            wait_for(grad_out[p].at[pl.ds(0, 2 if key[-1] == 1 else 1), pl.ds(key[2] * 4, 4)], sem)
        else:
            wait_for(grad_out[p].at[pl.ds(0, 4)], sem)

    def picked(buf, r):
        return jnp.concatenate([buf[lax.div(pats[r, j], 2), lax.rem(pats[r, j], 2)] for j in range(K)], axis=1)

    def whole(ref):
        return jnp.concatenate([ref[r] for r in range(HR)], axis=1)

    nt = (((1,), (1,)), ((), ()))

    def compute(key):
        kind = key[0]
        if kind == "load":
            for c in load_pat:
                c.wait()
            cols = lax.broadcasted_iota(jnp.int32, (HR, BLK), 1)
            inv = jnp.full((HR, BLK), K, jnp.int32)
            for j in range(K):
                inv = jnp.where(patv[:, j : j + 1] == cols, j, inv)
            invv[...] = inv
            load_inv.start()
            load_w1.wait()
            load_w2.wait()
            load_inv.wait()
            for w in (w1, w2):
                for r in range(HR):
                    w[r, K] = jnp.zeros((BLK, BLK), BF)
            return
        i = key[1]
        if kind in ("out", "back"):

            per = NX // OPT["np"]

            @pl.loop(key[2] * per, key[2] * per + per)
            def _(dx):
                dest = lax.rem(x + dx, NX) * NZ + lax.rem(z + (i + NZ), NZ)
                if kind == "out":
                    rhs = jnp.concatenate(
                        [
                            jnp.concatenate([w2[r, invs[r, 2 * dest + h]] for r in range(HR)], axis=0)
                            for h in (0, 1)
                        ],
                        axis=1,
                    )
                    res = jnp.dot(whole(act), rhs, preferred_element_type=F32)
                else:
                    rhs = jnp.concatenate(
                        [
                            jnp.concatenate([w1[r, invs[r, 2 * dest + h]] for r in range(HR)], axis=1)
                            for h in (0, 1)
                        ],
                        axis=0,
                    )
                    res = lax.dot_general(whole(pgrad), rhs, nt, preferred_element_type=F32)
                buf = part0 if kind == "out" else part1
                for h in (0, 1):
                    buf[dest, h] = res[:, h * BLK : (h + 1) * BLK].astype(BF)

            return

        @pl.loop(i * 2, i * 2 + 2)
        def _(n):
            r = lax.rem((1 - core) * 4 + n, HR)
            if kind == "pre":
                weights = jnp.concatenate([w1[r, j] for j in range(K)], axis=0)
                pre = jnp.dot(picked(xb, r), weights, preferred_element_type=F32)
                value, slope = gelu_pair(pre)
                act[r] = value.astype(BF)
                slope_ref[r] = slope
            elif kind == "sterm":
                res = jnp.dot(act[r].T, picked(gb, r), preferred_element_type=F32)
                for j in range(K):
                    sgr[r, j] = res[:, j * BLK : (j + 1) * BLK].astype(BF)
            elif kind == "agrad":
                weights = jnp.concatenate([w2[r, j] for j in range(K)], axis=1)
                res = lax.dot_general(picked(gb, r), weights, nt, preferred_element_type=F32)
                pgrad[r] = (res * slope_ref[r]).astype(BF)
            elif kind == "fterm":
                res = jnp.dot(pgrad[r].T, picked(xb, r), preferred_element_type=F32)
                for j in range(K):
                    fgr[r, j] = res[:, j * BLK : (j + 1) * BLK].astype(BF).T

    stores = []

    def store(src, dst):
        c = pltpu.make_async_copy(src, dst, local_sem.at[9 + len(stores)])
        c.start()
        stores.append(c)

    def marked(key):
        if key == ("gate", "ag", 1):
            for c in local[2:]:
                c.wait()
        if key[0] == "store":
            q = key[1]
            dst = (out_ref, back_ref)[q]
            for h in (0, 1):
                dst[:, h * BLK : (h + 1) * BLK] = parts[q][t, h]
        elif key[0] == "own":
            m, js = key[1], pl.ds(key[2] * 4, 4)
            store(grad_of[m].at[yrow(0), js], grad_out[m].at[yrow(0), js])

    for action, key in ORDER:
        if action == "send":
            copy_of(key).start()
        elif action == "recv":
            received(key)
        elif action == "comp":
            compute(key)
        else:
            marked(key)
    for p in (0, 1):
        if p in SENT["ag"]:
            wait_for(gathered[p].at[pl.ds(0, 31)], send_sem.at[SEND["ag"] + p], True)
        if p in SENT["rs"]:
            wait_for(parts[p].at[pl.ds(0, 31)], send_sem.at[SEND["rs"] + p], True)
        if p in SENT["ar"]:
            wait_for(grad_of[p].at[pl.ds(0, 7)], send_sem.at[SEND["yr"] + p], True)
            wait_for(grad_of[p].at[pl.ds(0, 7)], send_sem.at[SEND["yg"] + p], True)
    for c in stores:
        c.wait()


def finish(*refs):
    srcs, dsts, sem = refs[:4], refs[4:8], refs[8]
    copies = [pltpu.make_async_copy(src, dst, sem.at[i]) for i, (src, dst) in enumerate(zip(srcs, dsts))]
    for c in copies:
        c.start()
    for c in copies:
        c.wait()


def shards(tokens, pattern, first_blocks, second_blocks, out_grad):
    any_space = pl.BlockSpec(memory_space=pltpu.HBM)
    n = NSEM
    shapes = (
            jax.ShapeDtypeStruct(tokens.shape, BF),
            jax.ShapeDtypeStruct(tokens.shape, BF),
            jax.ShapeDtypeStruct(first_blocks.shape, BF),
            jax.ShapeDtypeStruct(second_blocks.shape, BF),
        )
    results = pl.pallas_call(
        kernel,
        out_shape=tuple(pltpu.VMEM(r.shape, BF) for r in shapes),
        in_specs=[
            any_space,
            any_space,
            any_space,
            any_space,
            any_space,
        ],
        out_specs=(pl.BlockSpec(memory_space=pltpu.VMEM),) * 4,
        scratch_shapes=[
            pltpu.VMEM((32, 2, ROWS, BLK), BF),
            pltpu.VMEM((32, 2, ROWS, BLK), BF),
            pltpu.VMEM((32, 2, ROWS, BLK), BF),
            pltpu.VMEM((32, 2, ROWS, BLK), BF),
            pltpu.VMEM((2, NA, 2, RA, BLK), BF),
            pltpu.VMEM((2, NB, 2, RB, BLK), BF),
            pltpu.VMEM((HR, K + 1, BLK, BLK), BF),
            pltpu.VMEM((HR, K + 1, BLK, BLK), BF),
            pltpu.VMEM((HR, ROWS, BLK), BF),
            pltpu.VMEM((HR, ROWS, BLK), BF),
            pltpu.VMEM((HR, ROWS, BLK), F32),
            pltpu.VMEM((HR, K, BLK, BLK), BF),
            pltpu.VMEM((HR, K, BLK, BLK), BF),
            pltpu.VMEM((2, 4, K, BLK, BLK), BF),
            pltpu.VMEM((2, NYS, K, BLK, BLK), BF),
            pltpu.VMEM((HR, K), jnp.int32),
            pltpu.SMEM((HR, K), jnp.int32),
            pltpu.VMEM((HR, BLK), jnp.int32),
            pltpu.SMEM((HR, BLK), jnp.int32),
            pltpu.SemaphoreType.DMA((8,)),
            pltpu.SemaphoreType.DMA((n,)),
            pltpu.SemaphoreType.DMA((13,)),
        ],
        compiler_params=pltpu.CompilerParams(
            collective_id=0, has_side_effects=True, vmem_limit_bytes=62500000
        ),
    )(tokens, out_grad, pattern, first_blocks, second_blocks)
    return pl.pallas_call(
        finish,
        out_shape=shapes,
        in_specs=[pl.BlockSpec(memory_space=pltpu.VMEM)] * 4,
        out_specs=(any_space,) * 4,
        scratch_shapes=[pltpu.SemaphoreType.DMA((4,))],
        compiler_params=pltpu.CompilerParams(vmem_limit_bytes=4 * 1024 * 1024),
    )(*[pltpu.with_memory_space_constraint(r, pltpu.VMEM) for r in results])


def solution(mesh):
    placed = (
        P("dp", "tensor"),
        P("tensor", None),
        P("tensor", None, None, None),
        P("tensor", None, None, None),
        P("dp", "tensor"),
    )
    return jax.shard_map(
        shards,
        mesh=mesh,
        in_specs=placed,
        out_specs=(
            P("dp", "tensor"),
            P("dp", "tensor"),
            P("tensor", None, None, None),
            P("tensor", None, None, None),
        ),
        check_vma=False,
    )
```

```python
import heapq
import random

import jax
import jax.numpy as jnp
from jax import lax
from jax.experimental import pallas as pl
from jax.experimental.pallas import tpu as pltpu
from jax.sharding import PartitionSpec as P

MESH = pl.DeviceIdType.MESH
BF = jnp.bfloat16
F32 = jnp.float32

gelu_scale = 0.7978845608028654
gelu_cube = 0.044715

NX, NZ, NY = 4, 8, 4
ROWS, BLK, HR, K = 256, 128, 8, 8
SIGNS = (1, -1)


OPT = dict(
    ra=(80, 112, 112, 96),
    UNIT=2.75,
    LAT=2.5,
    TH=1.5,
    PH=30,
    np=1,
    seed=4972,
    amp=4,
    y=0.93,
    g1=4,
    g2=52,
    g3=32,
    dzs=(4, 3, -3, 2, -2, 1, -1, 0),
    dxs=(2, 1, -1, 0),
    pf=0,
    ps=-1,
    cl=0.8,
    h=16,
    late_dx=(),
    late_dz=(0,),
)
SPLIT = OPT["ra"]
RA, RB = max(SPLIT), ROWS - min(SPLIT)
GROUP = {k: "ag" for k in ("ax", "az", "bz", "bx")} | {k: "rs" for k in ("rz", "rx", "sx", "sz")}
COST = {"ag": 0.03, "rs": 0.16}


def name(axis, s):
    return axis + ("+" if s > 0 else "-")


DZ=(4,3,-3,2,-2,1,-1,0)
def nz(dz): return 4 if dz==-4 else dz
def pair_of(key):
    if key[0]=="pc": return key
    if key[0]=="cg": return key[:2]
    return key[:-2]+key[-1:]
def recv_need(key):
    kind="out" if key[1]==0 else "back"
    if key[0] in ("rz","sz"): return [(kind, nz(c*(key[-1]-1))) for c in SIGNS]
    if key[0]=="rx": return [(kind,0)]
    if key[0]=="sx": return [(kind,key[2])]
    if key[0]=="pc": return [("grad",key[1],2)]
    return []
def build_items(o):
    items={}
    def add(key, link, size, deps): items[key]=(link,size,tuple(deps))
    for p in (0, 1):
        gate = [("gate", "ag", p)]
        fa = o["ra"][p] / ROWS
        fb = 1 - fa
        for s in SIGNS:
            add(("bz", p, s, 1), name("z", s), fb, gate)
            add(("ax", p, s, 1), name("x", s), fa, gate)
        for s in SIGNS:
            add(("az", p, 0, s, 1), name("z", s), fa, gate)
            add(("bx", p, 0, s, 1), name("x", s), fb, gate)
        for s in SIGNS:
            add(("ax", p, s, 2), name("x", s), fa / 2, [("ax", p, s, 1)])
            for k in (2, 3, 4):
                add(("bz", p, s, k), name("z", s), fb if k < 4 else fb / 2, [("bz", p, s, k - 1)])
        for dx, ready in ((0, gate),(-1, [("ax", p, 1, 1)]),(1, [("ax", p, -1, 1)]),(2, [("ax", p, 1, 2), ("ax", p, -1, 2)])):
            for s in SIGNS:
                for k in (1, 2, 3, 4):
                    add(("az", p, dx, s, k), name("z", s), fa if k < 4 else fa / 2, ready if k == 1 else [("az", p, dx, s, k - 1)])
        for dz in (0, -1, 1, -2, 2, -3, 3, 4):
            if dz == 0: ready = gate
            elif dz == 4: ready = [("bz", p, 1, 4), ("bz", p, -1, 4)]
            else: ready = [("bz", p, 1 if dz < 0 else -1, abs(dz))]
            for s in SIGNS:
                add(("bx", p, dz, s, 1), name("x", s), fb, ready)
                add(("bx", p, dz, s, 2), name("x", s), fb / 2, [("bx", p, dz, s, 1)])
    for q in (0, 1):
        kd="out" if q==0 else "back"
        fa = o["ra"][2 + q] / ROWS
        fb = 1 - fa
        def gate(c): return [("gate","rs",q)] + ([("gate2","rs",q)] if c else [])
        def done_a(dx): return [("rz", q, dx, s, 1) for s in SIGNS]
        def done_b(dz): return [("sx", q, dz, s, 1) for s in SIGNS]
        for dx in o["dxs"]:
            for s in SIGNS:
                for k in (4, 3, 2, 1):
                    add(("rz", q, dx, s, k), name("z", s), fa if k < 4 else fa / 2, (gate(dx in o.get("late_dx",())) if k == 4 else [("rz", q, dx, s, k + 1)])+[(kd,nz(s*k))])
        for dz in o["dzs"]:
            for s in SIGNS:
                add(("sx", q, dz, s, 2), name("x", s), fb / 2, gate(dz in o.get("late_dz",()))+[(kd,dz)])
                add(("sx", q, dz, s, 1), name("x", s), fb, [("sx", q, dz, s, 2)])
        for s in SIGNS:
            add(("rx", q, s, 2), name("x", s), fa / 2, done_a(2))
            add(("rx", q, s, 1), name("x", s), fa, [("rx", q, s, 2)] + done_a(s))
            add(("sz", q, s, 4), name("z", s), fb / 2, done_b(4))
            for k in (3, 2, 1):
                add(("sz", q, s, k), name("z", s), fb, [("sz", q, s, k + 1)] + done_b(s * k))
    for m in (0, 1):
        for v in (0,1):
            add(("pc", m, v), "c", o["cl"]/2, [("grad", m, v)])
        pcs=[("pc",m,0),("pc",m,1),("grad",m,2)]
        for u in (0,1):
            for s in SIGNS:
                add(("yr", m, u, s, 2), name("y", s), 0.5, pcs)
                add(("yr", m, u, s, 1), name("y", s), 1.0, [("yr", m, u, s, 2)])
        for u in (0,1):
            fin = [("yr", m, u, s, 1) for s in SIGNS]
            for s in SIGNS:
                add(("yg", m, u, s, 1), name("y", s), 1.0, fin)
                add(("yg", m, u, s, 2), name("y", s), 0.5, [("yg", m, u, s, 1)])
            add(("cg", m, u, 0), "c", 0.2, fin)
            add(("cg", m, u, -1), "c", 0.2, [("yg", m, u, 1, 1)])
            add(("cg", m, u, 1), "c", 0.2, [("yg", m, u, -1, 1)])
            add(("cg", m, u, 2), "c", 0.2, [("yg", m, u, 1, 2), ("yg", m, u, -1, 2)])
    return items
def build_chunks(o, items):
    def all_of(kinds, p): return [k for k in items if k[0] in kinds and k[1] == p]
    ag = ("ax", "az", "bz", "bx")
    chunks = [(("load",), 0.3, [("count", "ag", 0, 30)])]
    chunks += [(("pre", i), 0.56, all_of(ag, 0) + [("load",)]) for i in range(4)]
    pre = [("pre", i) for i in range(4)]
    np=o["np"]; chunks += [(("out", dz, c), 10.0/8/np, pre) for dz in o["dzs"] for c in range(np)]
    agr = [("agrad", i) for i in range(4)]
    tail=[(("back",dz,c),10.6/8/np,agr) for dz in o["dzs"] for c in range(np)]
    ft=[(("fterm",i),.63,agr) for i in range(4)]
    st=[(("sterm",i),.5,all_of(ag,1)+pre) for i in range(4)]
    tail[o["pf"]:o["pf"]]=ft
    ps=o["ps"]
    if ps>=0: tail[ps:ps]=st
    ag_=[(("agrad",i),.55,all_of(ag,1)+pre) for i in range(4)]
    chunks += (st if ps<0 else [])+ag_+tail
    return chunks
def build_marks(o, items):
    final = [[("rx", q, s, 1) for s in SIGNS]+ [("rz", q, 0, s, 1) for s in SIGNS]+ [("sz", q, s, 1) for s in SIGNS]+ [("sx", q, 0, s, 1) for s in SIGNS] for q in (0, 1)]
    marks = [
        (("gate", "ag", 0), []),
        (("gate", "ag", 1), [("count", "ag", 0, o["g1"])]),
        (("gate", "rs", 0), [("count", "ag", 1, o["g2"])]),
        (("gate", "rs", 1), [("count", "rs", 0, o["g3"])]),
        (("gate2", "rs", 0), [("count", "rs", 0, o.get("h",0))]),
        (("gate2", "rs", 1), [("count", "rs", 1, o.get("h",0))]),
        (("store", 0), final[0]),(("store", 1), final[1]),
    ]
    for kd in ("out","back"):
        marks += [((kd,dz),[(kd,dz,c) for c in range(o["np"])]) for dz in DZ]
    for m,n in ((0,"sterm"),(1,"fterm")):
        marks += [(("grad", m, 0), [(n,0)]),(("grad", m, 1), [(n,1)]),(("grad", m, 2), [(n,i) for i in range(4)])]
        for u in (0,1): marks.append((("own",m,u),[("yr",m,u,s,1) for s in SIGNS]))
    return marks
def ranks(o, items):
    after={}
    for k,(_,_,deps) in items.items():
        for d in deps: after.setdefault(d,[]).append(k)
    left={}
    def way(k):
        if k not in left: left[k]=items[k][1]*o["UNIT"]+o["LAT"]+max([way(n) for n in after.get(k,[])]+[0.0])
        return left[k]
    def phase(k):
        g=GROUP.get(k[0],"ar")
        return k[1] if g=="ag" else 2+k[1] if g=="rs" else k[1]
    rnd=random.Random(o["seed"])
    return {k:(phase(k)*o["PH"]-way(k)+o["amp"]*rnd.random(),i) for i,k in enumerate(items)}
def build_order(o):
    items = build_items(o); chunks = build_chunks(o, items); marks = build_marks(o, items)
    UNIT,LAT=o["UNIT"],o["LAT"]
    got, counts, free = set(), {}, {}
    waiting = list(items); heap, order = [], []; now, seq = 0.0, 0
    pend={}; members={}; ready=[]; rank=ranks(o, items)
    for k in items: members[pair_of(k)]=members.get(pair_of(k),0)+1
    def met(need):
        if need[0] == "count": return counts.get((need[1], need[2]), 0) >= need[3]
        return need in got
    def settle():
        nonlocal now, seq
        moved = True
        while moved:
            moved = False
            for mark in list(marks):
                if all(met(n) for n in mark[1]):
                    marks.remove(mark); order.append(("mark", mark[0])); got.add(mark[0]); moved = True
            for key in list(waiting):
                if all(d in got for d in items[key][2]):
                    waiting.remove(key); ready.append(key)
            ready.sort(key=lambda k: rank[k])
            for key in list(ready):
                link, size, _ = items[key]
                if free.get(link, 0.0) - now < o["TH"]:
                    ready.remove(key); order.append(("send", key)); now += 0.03
                    start = max(now, free.get(link, 0.0))
                    free[link] = start + size * UNIT * o.get(link[0], 1.0); seq += 1
                    pair=pair_of(key); pend.setdefault(pair,[]).append(free[link]+LAT)
                    if len(pend[pair])==members[pair]: heapq.heappush(heap, (max(pend[pair]), seq, pair))
                    moved = True
    settle()
    held=[]
    while heap or chunks or held:
        key=None
        for h in held:
            if all(n in got for n in recv_need(h)): key=h; held.remove(h); break
        if key is None and heap and heap[0][0] <= now:
            key = heapq.heappop(heap)[2]
            if not all(n in got for n in recv_need(key)): held.append(key); continue
        if key is not None:
            order.append(("recv", key)); got.update(k for k in items if pair_of(k)==key)
            group = GROUP.get(key[0], "ar"); counts[(group, key[1])] = counts.get((group, key[1]), 0) + members[key]
            now += COST.get(group, 0.2); settle(); continue
        if chunks and all(met(n) for n in chunks[0][2]):
            key, time, _ = chunks.pop(0); order.append(("comp", key)); got.add(key); now += time
            settle(); continue
        if not heap: return None
        now = max(now, heap[0][0])
    if waiting or marks or ready: return None
    return list(items), order, now


KEYS, ORDER, SPAN = build_order(OPT)
PAIRS = list(dict.fromkeys(pair_of(k) for k in KEYS))


def semaphore_index():
    index, n = {}, {}
    for k in PAIRS:
        group = GROUP.get(k[0], "ar")
        slot = (group, k[1] if group != "ar" else 0)
        index[k] = n.get(slot, 0) + (76 if group == "ar" else 38 * k[1])
        n[slot] = n.get(slot, 0) + 1
    return index, max(index.values()) + 1


INDEX, NSEM = semaphore_index()


def slot_index():
    a, b, y = {}, {}, {}
    na = nb = ny = 0
    for k in PAIRS:
        split = k[-1] == (4 if k[0][-1] == "z" else 2)
        n = 1 if split else 2
        if k[0] in ("rz", "rx") and k[1] == 0:
            a[(k[0],) + k[2:]] = na
            na += n
        if k[0] in ("sx", "sz") and k[1] == 0:
            b[(k[0],) + k[2:]] = nb
            nb += n
        if k[0] == "yr" and k[1:3] == (0, 0):
            y[k[-1]] = ny
            ny += n
    return a, b, y, na, nb, ny


SLOT_A, SLOT_B, SLOT_Y, NA, NB, NYS = slot_index()
SENT = {"ag": (0, 1), "rs": (0, 1), "ar": (0, 1)}
SEND = {"ag": 0, "rs": 2, "pc": 4, "yr": 4, "yg": 6, "cg": 6}


def gelu_pair(value):
    inner = gelu_scale * (value + gelu_cube * value * value * value)
    tangent = jnp.tanh(inner)
    result = 0.5 * value * (1.0 + tangent)
    slope = 0.5 * (1.0 + tangent) + 0.5 * value * (1.0 - tangent * tangent) * gelu_scale * (
        1.0 + 3.0 * gelu_cube * value * value
    )
    return result, slope


def kernel(
    tokens, grads, pattern, first, second,
    out_ref, back_ref, fgrad_ref, sgrad_ref,
    xb, gb, part0, part1, slot_a, slot_b, w1, w2, act, pgrad, slope_ref,
    sgr, fgr, pair, yslot, patv, pats, invv, invs,
    send_sem, recv_sem, local_sem,
):
    t = lax.axis_index("tensor")
    d = lax.axis_index("dp")
    x, z = lax.div(t, NZ), lax.rem(t, NZ)
    y, core = lax.div(d, 2), lax.rem(d, 2)

    def at(dx, dz):
        return lax.rem(x + (dx + NX), NX) * NZ + lax.rem(z + (dz + NZ), NZ)

    def dev_x(s):
        return {"tensor": at(s, 0)}

    def dev_z(s):
        return {"tensor": at(0, s)}

    def dev_y(s):
        return {"dp": lax.rem(y + (s + NY), NY) * 2 + core}

    partner = {"dp": y * 2 + (1 - core)}
    base = core * 4

    def yrow(dy, b=None):
        return (base if b is None else b) + lax.rem(y + (dy + NY), NY)

    local = []
    for n, (src, buf) in enumerate(((tokens, xb), (grads, gb))):
        for h in (0, 1):
            c = pltpu.make_async_copy(
                src.at[:, pl.ds(h * BLK, BLK)], buf.at[t, h], local_sem.at[2 * n + h]
            )
            if n == 0:
                c.start()
            local.append(c)
    load_w1 = pltpu.make_async_copy(first, w1.at[:, pl.ds(0, K)], local_sem.at[4])
    load_w2 = pltpu.make_async_copy(second, w2.at[:, pl.ds(0, K)], local_sem.at[5])
    load_pat = [
        pltpu.make_async_copy(pattern, patv, local_sem.at[7]),
        pltpu.make_async_copy(pattern, pats, local_sem.at[8]),
    ]

    load_inv = pltpu.make_async_copy(invv, invs, local_sem.at[6])
    barrier = pltpu.get_barrier_semaphore()
    for dev in (dev_x(1), dev_x(-1), dev_z(1), dev_z(-1), dev_y(1), dev_y(-1), partner):
        pl.semaphore_signal(barrier, inc=1, device_id=dev, device_id_type=MESH)


    for c in local[:2]:
        c.wait()
    pl.semaphore_wait(barrier, 7)
    for c in local[2:] + load_pat + [load_w1, load_w2]:
        c.start()

    gathered = (xb, gb)
    parts = (part0, part1)
    grad_of = (sgr, fgr)
    grad_out = (sgrad_ref, fgrad_ref)

    def rows_of(key):
        n = SPLIT[key[1] + (0 if GROUP[key[0]] == "ag" else 2)]
        return (pl.ds(0, n), n) if key[0][0] in "ar" else (pl.ds(n, ROWS - n), ROWS - n)

    def half(s):
        return 0 if s > 0 else 1

    def reduce_slot(key):
        rows, n = rows_of(key)
        kind, q, s, k = key[0], key[1], key[-2], key[-1]
        sub = (kind,) + key[2:-2] + (k,)
        split = k == (4 if kind[1] == "z" else 2)
        lane = 0 if split or s > 0 else 1
        if kind[0] == "r":
            return rows, slot_a.at[q, SLOT_A[sub] + lane, :, pl.ds(0, n), :], split
        return rows, slot_b.at[q, SLOT_B[sub] + lane, :, pl.ds(0, n), :], split

    def reduce_shard(key, k):
        kind, s = key[0], key[-2]
        if kind == "rz":
            return at(key[2], s * k)
        if kind == "sz":
            return at(0, s * k)
        if kind == "rx":
            return at(s * k, 0)
        return at(s * k, key[2])

    def copy_of(key):
        kind, p = key[0], key[1]
        group = GROUP.get(kind, kind)
        ss, rs = send_sem.at[SEND[group] + p], recv_sem.at[INDEX[pair_of(key)]]

        def remote(src, dst, dev):
            return pltpu.make_async_remote_copy(
                src_ref=src, dst_ref=dst, send_sem=ss, recv_sem=rs, device_id=dev, device_id_type=MESH
            )

        if group == "ag":
            s, k = key[-2], key[-1]
            rows = rows_of(key)[0]
            if kind == "ax":
                own, dev, split = at(-s * (k - 1), 0), dev_x(s), k == 2
            elif kind == "az":
                own, dev, split = at(key[2], -s * (k - 1)), dev_z(s), k == 4
            elif kind == "bz":
                own, dev, split = at(0, -s * (k - 1)), dev_z(s), k == 4
            else:
                own, dev, split = at(-s * (k - 1), key[2]), dev_x(s), k == 2
            view = gathered[p].at[own, pl.ds(half(s), 1) if split else pl.ds(0, 2), rows, :]
            return remote(view, view, dev)
        if group == "rs":
            s, k = key[-2], key[-1]
            rows, slot, split = reduce_slot(key)
            hs = pl.ds(half(s), 1) if split else pl.ds(0, 2)
            dev = dev_z(s) if kind[1] == "z" else dev_x(s)
            return remote(parts[p].at[reduce_shard(key, k), hs, rows, :], slot.at[hs], dev)
        g, out = grad_of[p], grad_out[p]
        if kind == "pc":
            v = key[2] * 2
            return remote(g.at[pl.ds((1 - core) * 4 + v, 2)], pair.at[p, pl.ds(v, 2)], partner)
        u, s, k = key[2] * 4, key[-2], key[-1]
        if kind == "cg":
            js, dy = pl.ds(u, 4), key[3]
            src = g.at[yrow(0), js] if dy == 0 else out.at[yrow(dy), js]
            return remote(src, out.at[yrow(dy), js], partner)
        js = pl.ds(u + half(s) * 2, 2) if k == 2 else pl.ds(u, 4)
        if kind == "yr":
            slot = SLOT_Y[k] + (0 if k == 2 or s > 0 else 1)
            return remote(g.at[yrow(s * k), js], yslot.at[p, slot, js], dev_y(s))
        src = g.at[yrow(0), js] if k == 1 else out.at[yrow(-s), js]
        return remote(src, out.at[yrow(-s * (k - 1)), js], dev_y(s))

    def wait_for(view, sem, sent=False):
        c = pltpu.make_async_remote_copy(
            src_ref=view, dst_ref=view, send_sem=sem, recv_sem=sem, device_id=partner, device_id_type=MESH
        )
        if sent:
            c.wait_send()
        else:
            c.wait_recv()

    def received(key):
        kind, p = key[0], key[1]
        sem = recv_sem.at[INDEX[key]]
        group = GROUP.get(kind, kind)
        if group == "ag":
            rows = rows_of(key)[0]
            split = key[-1] == (4 if kind[1] == "z" else 2)
            wait_for(gathered[p].at[pl.ds(0, 1 if split else 2), :, rows, :], sem)
        elif group == "rs":
            split = key[-1] == (4 if kind[1] == "z" else 2)
            signed = [key[:-1] + (s, key[-1]) for s in SIGNS]
            rows = rows_of(key)[0]
            wait_for(parts[p].at[pl.ds(0, 1 if split else 2), :, rows, :], sem)
            places = [reduce_shard(k, key[-1] - 1) for k in signed]
            slots = [reduce_slot(k)[1] for k in signed]
            if key[-1] == 1:
                for h in (0, 1):
                    total = parts[p][places[0], h, rows, :].astype(F32)
                    total = total + slots[0][h].astype(F32) + slots[1][h].astype(F32)
                    parts[p][places[0], h, rows, :] = total.astype(BF)
                return
            for s, mine, slot in zip(SIGNS, places, slots):
                for h in (half(s),) if split else (0, 1):
                    parts[p][mine, h, rows, :] = parts[p][mine, h, rows, :] + slot[h]
        elif kind == "pc":
            v = key[2] * 2
            g = grad_of[p]
            wait_for(pair.at[p, pl.ds(v, 2)], sem)

            @pl.loop(v, v + 2)
            def _(r):
                @pl.loop(0, K)
                def _(j):
                    total = g[base + r, j] + pair[p, r, j]
                    g[base + r, j] = total
        elif kind == "yr":
            u, k = key[2] * 4, key[-1]
            g = grad_of[p]
            if k == 2:
                wait_for(yslot.at[p, SLOT_Y[2], pl.ds(u, 4)], sem)
                for s in SIGNS:
                    row = yrow(s)
                    lo = u + half(s) * 2

                    @pl.loop(lo, lo + 2)
                    def _(j):
                        total = g[row, j] + yslot[p, SLOT_Y[2], j]
                        g[row, j] = total
            else:
                wait_for(yslot.at[p, pl.ds(SLOT_Y[1], 2), pl.ds(u, 4)], sem)
                row = yrow(0)

                @pl.loop(u, u + 4)
                def _(j):
                    total = g[row, j].astype(F32) + yslot[p, SLOT_Y[1], j].astype(F32)
                    total = total + yslot[p, SLOT_Y[1] + 1, j].astype(F32)
                    g[row, j] = total.astype(BF)
        elif kind == "yg":
            wait_for(grad_out[p].at[pl.ds(0, 2 if key[-1] == 1 else 1), pl.ds(key[2] * 4, 4)], sem)
        else:
            wait_for(grad_out[p].at[pl.ds(0, 4)], sem)

    def picked(buf, r):
        return jnp.concatenate([buf[lax.div(pats[r, j], 2), lax.rem(pats[r, j], 2)] for j in range(K)], axis=1)

    def whole(ref):
        return jnp.concatenate([ref[r] for r in range(HR)], axis=1)

    nt = (((1,), (1,)), ((), ()))

    def compute(key):
        kind = key[0]
        if kind == "load":
            for c in load_pat:
                c.wait()
            cols = lax.broadcasted_iota(jnp.int32, (HR, BLK), 1)
            inv = jnp.full((HR, BLK), K, jnp.int32)
            for j in range(K):
                inv = jnp.where(patv[:, j : j + 1] == cols, j, inv)
            invv[...] = inv
            load_inv.start()
            load_w1.wait()
            load_w2.wait()
            load_inv.wait()
            for w in (w1, w2):
                for r in range(HR):
                    w[r, K] = jnp.zeros((BLK, BLK), BF)
            return
        i = key[1]
        if kind in ("out", "back"):

            per = NX // OPT["np"]

            @pl.loop(key[2] * per, key[2] * per + per)
            def _(dx):
                dest = lax.rem(x + dx, NX) * NZ + lax.rem(z + (i + NZ), NZ)
                if kind == "out":
                    rhs = jnp.concatenate(
                        [
                            jnp.concatenate([w2[r, invs[r, 2 * dest + h]] for r in range(HR)], axis=0)
                            for h in (0, 1)
                        ],
                        axis=1,
                    )
                    res = jnp.dot(whole(act), rhs, preferred_element_type=F32)
                else:
                    rhs = jnp.concatenate(
                        [
                            jnp.concatenate([w1[r, invs[r, 2 * dest + h]] for r in range(HR)], axis=1)
                            for h in (0, 1)
                        ],
                        axis=0,
                    )
                    res = lax.dot_general(whole(pgrad), rhs, nt, preferred_element_type=F32)
                buf = part0 if kind == "out" else part1
                for h in (0, 1):
                    buf[dest, h] = res[:, h * BLK : (h + 1) * BLK].astype(BF)

            return

        @pl.loop(i * 2, i * 2 + 2)
        def _(n):
            r = lax.rem((1 - core) * 4 + n, HR)
            if kind == "pre":
                weights = jnp.concatenate([w1[r, j] for j in range(K)], axis=0)
                pre = jnp.dot(picked(xb, r), weights, preferred_element_type=F32)
                value, slope = gelu_pair(pre)
                act[r] = value.astype(BF)
                slope_ref[r] = slope
            elif kind == "sterm":
                res = jnp.dot(act[r].T, picked(gb, r), preferred_element_type=F32)
                for j in range(K):
                    sgr[r, j] = res[:, j * BLK : (j + 1) * BLK].astype(BF)
            elif kind == "agrad":
                weights = jnp.concatenate([w2[r, j] for j in range(K)], axis=1)
                res = lax.dot_general(picked(gb, r), weights, nt, preferred_element_type=F32)
                pgrad[r] = (res * slope_ref[r]).astype(BF)
            elif kind == "fterm":
                res = jnp.dot(pgrad[r].T, picked(xb, r), preferred_element_type=F32)
                for j in range(K):
                    fgr[r, j] = res[:, j * BLK : (j + 1) * BLK].astype(BF).T

    stores = []

    def store(src, dst):
        c = pltpu.make_async_copy(src, dst, local_sem.at[9 + len(stores)])
        c.start()
        stores.append(c)

    def marked(key):
        if key == ("gate", "ag", 1):
            for c in local[2:]:
                c.wait()
        if key[0] == "store":
            q = key[1]
            dst = (out_ref, back_ref)[q]
            for h in (0, 1):
                dst[:, h * BLK : (h + 1) * BLK] = parts[q][t, h]
        elif key[0] == "own":
            m, js = key[1], pl.ds(key[2] * 4, 4)
            store(grad_of[m].at[yrow(0), js], grad_out[m].at[yrow(0), js])

    for action, key in ORDER:
        if action == "send":
            copy_of(key).start()
        elif action == "recv":
            received(key)
        elif action == "comp":
            compute(key)
        else:
            marked(key)
    for p in (0, 1):
        if p in SENT["ag"]:
            wait_for(gathered[p].at[pl.ds(0, 31)], send_sem.at[SEND["ag"] + p], True)
        if p in SENT["rs"]:
            wait_for(parts[p].at[pl.ds(0, 31)], send_sem.at[SEND["rs"] + p], True)
        if p in SENT["ar"]:
            wait_for(grad_of[p].at[pl.ds(0, 7)], send_sem.at[SEND["yr"] + p], True)
            wait_for(grad_of[p].at[pl.ds(0, 7)], send_sem.at[SEND["yg"] + p], True)
    for c in stores:
        c.wait()


def finish(*refs):
    srcs, dsts, sem = refs[:4], refs[4:8], refs[8]
    copies = [pltpu.make_async_copy(src, dst, sem.at[i]) for i, (src, dst) in enumerate(zip(srcs, dsts))]
    for c in copies:
        c.start()
    for c in copies:
        c.wait()


def shards(tokens, pattern, first_blocks, second_blocks, out_grad):
    any_space = pl.BlockSpec(memory_space=pltpu.HBM)
    n = NSEM
    shapes = (
            jax.ShapeDtypeStruct(tokens.shape, BF),
            jax.ShapeDtypeStruct(tokens.shape, BF),
            jax.ShapeDtypeStruct(first_blocks.shape, BF),
            jax.ShapeDtypeStruct(second_blocks.shape, BF),
        )
    results = pl.pallas_call(
        kernel,
        out_shape=tuple(pltpu.VMEM(r.shape, BF) for r in shapes),
        in_specs=[
            any_space,
            any_space,
            any_space,
            any_space,
            any_space,
        ],
        out_specs=(pl.BlockSpec(memory_space=pltpu.VMEM),) * 4,
        scratch_shapes=[
            pltpu.VMEM((32, 2, ROWS, BLK), BF),
            pltpu.VMEM((32, 2, ROWS, BLK), BF),
            pltpu.VMEM((32, 2, ROWS, BLK), BF),
            pltpu.VMEM((32, 2, ROWS, BLK), BF),
            pltpu.VMEM((2, NA, 2, RA, BLK), BF),
            pltpu.VMEM((2, NB, 2, RB, BLK), BF),
            pltpu.VMEM((HR, K + 1, BLK, BLK), BF),
            pltpu.VMEM((HR, K + 1, BLK, BLK), BF),
            pltpu.VMEM((HR, ROWS, BLK), BF),
            pltpu.VMEM((HR, ROWS, BLK), BF),
            pltpu.VMEM((HR, ROWS, BLK), F32),
            pltpu.VMEM((HR, K, BLK, BLK), BF),
            pltpu.VMEM((HR, K, BLK, BLK), BF),
            pltpu.VMEM((2, 4, K, BLK, BLK), BF),
            pltpu.VMEM((2, NYS, K, BLK, BLK), BF),
            pltpu.VMEM((HR, K), jnp.int32),
            pltpu.SMEM((HR, K), jnp.int32),
            pltpu.VMEM((HR, BLK), jnp.int32),
            pltpu.SMEM((HR, BLK), jnp.int32),
            pltpu.SemaphoreType.DMA((8,)),
            pltpu.SemaphoreType.DMA((n,)),
            pltpu.SemaphoreType.DMA((13,)),
        ],
        compiler_params=pltpu.CompilerParams(
            collective_id=0, has_side_effects=True, vmem_limit_bytes=62500000
        ),
    )(tokens, out_grad, pattern, first_blocks, second_blocks)
    return pl.pallas_call(
        finish,
        out_shape=shapes,
        in_specs=[pl.BlockSpec(memory_space=pltpu.VMEM)] * 4,
        out_specs=(any_space,) * 4,
        scratch_shapes=[pltpu.SemaphoreType.DMA((4,))],
        compiler_params=pltpu.CompilerParams(vmem_limit_bytes=4 * 1024 * 1024),
    )(*[pltpu.with_memory_space_constraint(r, pltpu.VMEM) for r in results])


def solution(mesh):
    placed = (
        P("dp", "tensor"),
        P("tensor", None),
        P("tensor", None, None, None),
        P("tensor", None, None, None),
        P("dp", "tensor"),
    )
    return jax.shard_map(
        shards,
        mesh=mesh,
        in_specs=placed,
        out_specs=(
            P("dp", "tensor"),
            P("dp", "tensor"),
            P("tensor", None, None, None),
            P("tensor", None, None, None),
        ),
        check_vma=False,
    )
```
